256 devices in a mesh: bx: 16 (over z, x_hi), by: 16 (over x_lo, y, core).
Axes of the slice: x: 4 (x_hi: 2, x_lo: 2; x = x_hi * 2 + x_lo), y: 4, z: 8, core: 2. Of those that a mesh axis runs over, the one named last changes fastest.
Arguments:
- features: float32 [16, 16, 128, 128], P('bx', 'by'), may hold values from -6 to 6
- send_list: int32 [16, 16, 4, 32], P('bx', 'by'), may hold values from 0 to 127, as said below
- pair_first: int32 [16, 16, 2048], P('bx', 'by'), may hold values from 0 to 127, as said below
- pair_second: int32 [16, 16, 2048], P('bx', 'by'), may hold values from 0 to 255, as said below
- pair_species: int32 [16, 16, 2048], P('bx', 'by'), may hold values from 0 to 15
- pair_vector: float32 [16, 16, 3, 2048], P('bx', 'by'), may hold values from -2.5 to 2.5
- live_pairs: int32 [16, 16], P('bx', 'by'), may hold values from 1024 to 2048, as said below
- force_target: float32 [16, 16, 3, 128], P('bx', 'by'), may hold values from -12 to 12
- w_a: float32 [128, 512], replicated, may hold values from -0.5 to 0.5
- w_b: float32 [128, 512], replicated, may hold values from -0.5 to 0.5
- w_radial: float32 [8, 512], replicated, may hold values from -6 to 6
- species_table: float32 [16, 512], replicated, may hold values from -3 to 3
- w_mid: float32 [512, 512], replicated, may hold values from -0.25 to 0.25
- w_out: float32 [512], replicated, may hold values from -0.25 to 0.25
Outputs:
- forces: float32 [16, 16, 3, 128], P('bx', 'by')
- grad_w_a: float32 [128, 512], replicated
- grad_w_b: float32 [128, 512], replicated
- grad_w_radial: float32 [8, 512], replicated
- grad_species_table: float32 [16, 512], replicated
- grad_w_mid: float32 [512, 512], replicated
- grad_w_out: float32 [512], replicated
The draws below stay inside these ranges and needn't reach their ends.
Inputs may be any that keep to these rules, and one draw needn't show every extreme that they name: `pair_first`: the first atom of a pair is a local atom of the brick. `pair_second`: below 128 a local atom other than the slot's first atom; 128 + d * 32 + g names ghost row g of direction d. `send_list`: for each brick and direction, 32 distinct local atoms. `live_pairs`: slots below it are live; in every draw some brick has all 2048 slots live.
All inputs are finite; a program needn't handle non-finite values.
Results may differ from the reference program's by a relative error of at most 0.0003.
Values sent between devices are 32-bit elements; how exact they have to be, the bound alone decides.
No kernel may reach another device: no remote copies, remote signals or barrier semaphores. Data moves between devices by JAX's collectives and lax.ppermute only.
A program may use at most 64 MiB of HBM per device.

```python
import math
import jax
import jax.numpy as jnp
from jax import lax

F = 128
H = 512
NB = 8
NS = 16
ATOM_DEV = 128
PAIR_DEV = 2048
GHOST = 32
N_BX = 16
N_BY = 16


def pair_atoms(key):
    base = jax.random.fold_in(key, 101)
    k_first, k_coin, k_slot, k_step = jax.random.split(base, 4)
    shape = (N_BX, N_BY, PAIR_DEV)
    first = jax.random.randint(k_first, shape, 0, ATOM_DEV)
    coin = jax.random.randint(k_coin, shape, 0, 2)
    slot = jax.random.randint(k_slot, shape, 0, 4 * GHOST)
    offset = jax.random.randint(k_step, shape, 1, ATOM_DEV)
    second = jnp.where(coin == 1, ATOM_DEV + slot, (first + offset) % ATOM_DEV)
    return (first.astype(jnp.int32), second.astype(jnp.int32))


def draw_pair_first(key, part):
    return pair_atoms(key)[0]


def draw_pair_second(key, part):
    return pair_atoms(key)[1]


def draw_send_list(key, part):
    scores = jax.random.randint(jax.random.fold_in(key, 202), (N_BX, N_BY, 4, ATOM_DEV), 0, 1 << 20)
    scores = scores * ATOM_DEV + jnp.arange(ATOM_DEV, dtype=jnp.int32)
    picked = jnp.argsort(scores, axis=-1, stable=True)[..., :GHOST]
    return picked.astype(jnp.int32)


def draw_live_pairs(key, part):
    k_count, k_pick = jax.random.split(jax.random.fold_in(key, 303))
    bricks = N_BX * N_BY
    counts = jax.random.randint(k_count, (bricks,), PAIR_DEV // 2, PAIR_DEV + 1)
    pick = jax.random.randint(k_pick, (), 0, bricks)
    counts = jnp.where(jnp.arange(bricks) == pick, PAIR_DEV, counts)
    return counts.reshape(N_BX, N_BY).astype(jnp.int32)


def place_ends(values, own_key, low, largest):
    dims = values.shape
    index_at = [jax.random.randint(jax.random.fold_in(own_key, axis), (), 0, dims[axis]) for axis in range(len(dims))]
    values = values.at[tuple(index_at)].set(low)
    longest = dims.index(max(dims))
    index_at[longest] = (index_at[longest] + 1) % dims[longest]
    return values.at[tuple(index_at)].set(largest)


def steps_of(rng, dims, cuts, smallest, largest):
    gain, own = 1.0, jax.random.fold_in(rng, 6)
    for axis_at, blocks in cuts:
        steps = jnp.exp(jax.random.uniform(jax.random.fold_in(own, axis_at), (blocks,), jnp.float32, smallest / len(cuts), largest / len(cuts)))
        gain = gain * jnp.repeat(steps, dims[axis_at] // blocks).reshape([-1 if axis == axis_at else 1 for axis in range(len(dims))])
    return gain


def noise(key, shape, deviation, bound, cuts=(), kind=jnp.bfloat16):
    gain = steps_of(key, shape, cuts, -0.22, 0.18) if cuts else 1.0
    result = jax.random.normal(key, shape, jnp.float32) * deviation * gain
    return jnp.minimum(jnp.maximum(result, -bound), bound).astype(kind)


def setup_inputs(seed: int = 0) -> dict:
    arg_keys = jax.random.split(jax.random.key(seed), 15)
    features = noise(arg_keys[0], (N_BX, N_BY, ATOM_DEV, F), 1.0, 6.0, ((0, 16), (1, 16)), jnp.float32)
    send_list = draw_send_list(jax.random.fold_in(arg_keys[14], 71), 0)
    pair_first = draw_pair_first(jax.random.fold_in(arg_keys[14], 71), 0)
    pair_second = draw_pair_second(jax.random.fold_in(arg_keys[14], 71), 0)
    pair_species = place_ends(jax.random.randint(arg_keys[4], (N_BX, N_BY, PAIR_DEV), 0, NS), jax.random.fold_in(arg_keys[4], 1), 0, NS - 1).astype(jnp.int32)
    pair_vector = jnp.clip(jax.random.uniform(arg_keys[5], (N_BX, N_BY, 3, PAIR_DEV), jnp.float32, -2.5, 2.5) * steps_of(arg_keys[5], (N_BX, N_BY, 3, PAIR_DEV), ((0, 16), (1, 16)), -0.4, 0.0), -2.5, 2.5)
    live_pairs = draw_live_pairs(jax.random.fold_in(arg_keys[14], 71), 0)
    force_target = noise(arg_keys[7], (N_BX, N_BY, 3, ATOM_DEV), 2.0, 12.0, ((0, 16), (1, 16)), jnp.float32)
    w_a = noise(arg_keys[8], (F, H), F ** -0.5, 0.5, (), jnp.float32)
    w_b = noise(arg_keys[9], (F, H), F ** -0.5, 0.5, (), jnp.float32)
    w_radial = noise(arg_keys[10], (NB, H), 1.0, 6.0, (), jnp.float32)
    species_table = noise(arg_keys[11], (NS, H), 0.5, 3.0, (), jnp.float32)
    w_mid = noise(arg_keys[12], (H, H), H ** -0.5, 0.25, (), jnp.float32)
    w_out = noise(arg_keys[13], (H,), H ** -0.5, 0.25, (), jnp.float32)
    return {"features": features, "send_list": send_list, "pair_first": pair_first, "pair_second": pair_second, "pair_species": pair_species, "pair_vector": pair_vector, "live_pairs": live_pairs, "force_target": force_target, "w_a": w_a, "w_b": w_b, "w_radial": w_radial, "species_table": species_table, "w_mid": w_mid, "w_out": w_out}


DIRS = ((1, 0), (0, 1), (1, 1), (1, -1))
RCUT = 5.0

def pair_slope(params, first_rows, second_rows, kinds, vec):
    w_a, w_b, w_radial, species_table, w_mid, w_out = params
    highest = lax.Precision.HIGHEST
    square = lax.optimization_barrier(jnp.sum(vec * vec, axis=0)) + 1.0
    radius = jnp.sqrt(square)
    order = (jnp.arange(1, w_radial.shape[0] + 1).astype(vec.dtype) * (math.pi / RCUT))[:, None]
    phase = order * radius[None, :]
    basis = jnp.sin(phase) / radius
    basis_slope = order * jnp.cos(phase) / radius - jnp.sin(phase) / square
    pre = jnp.dot(first_rows, w_a, precision=highest) + jnp.dot(second_rows, w_b, precision=highest)
    pre = pre + jnp.dot(basis.T, w_radial, precision=highest) + jnp.dot(kinds, species_table, precision=highest)
    sig_pre = jax.nn.sigmoid(pre)
    mid = jnp.dot(pre * sig_pre, w_mid, precision=highest)
    sig_mid = jax.nn.sigmoid(mid)
    grad_mid = w_out * sig_mid * (1.0 + mid * (1.0 - sig_mid))
    grad_pre = jnp.dot(grad_mid, w_mid.T, precision=highest) * sig_pre * (1.0 + pre * (1.0 - sig_pre))
    along = jnp.dot(grad_pre, w_radial.T, precision=highest)
    return lax.optimization_barrier(jnp.sum(along.T * basis_slope, axis=0)) / radius

def ghost_rows(table, send_list):
    pieces = []
    for d, (dx, dy) in enumerate(DIRS):
        source = jnp.roll(table, (-dx, -dy), axis=(0, 1))
        chosen = jnp.roll(send_list[:, :, d, :], (-dx, -dy), axis=(0, 1))
        pieces.append(jnp.take_along_axis(source, chosen[..., None], axis=2))
    return jnp.concatenate(pieces, axis=2)

def reference(features, send_list, pair_first, pair_second, pair_species, pair_vector, live_pairs, force_target, w_a, w_b, w_radial, species_table, w_mid, w_out):
    highest = lax.Precision.HIGHEST
    nbx, nby, atoms, width = features.shape
    ghosts = send_list.shape[3]
    pairs = pair_first.shape[2]
    extent = atoms + 4 * ghosts
    params = (w_a, w_b, w_radial, species_table, w_mid, w_out)
    table = jnp.concatenate([features, ghost_rows(features, send_list)], axis=2)
    flat_table = table.reshape(nbx * nby, extent, width)
    flat_first = pair_first.reshape(nbx * nby, pairs)
    flat_second = pair_second.reshape(nbx * nby, pairs)
    flat_species = pair_species.reshape(nbx * nby, pairs)
    flat_vec = pair_vector.reshape(nbx * nby, 3, pairs)
    flat_live = live_pairs.reshape(nbx * nby)
    columns = jnp.arange(extent)
    kinds_all = jnp.arange(species_table.shape[0])

    def brick_inputs(rows, fi, se, sp, live):
        kinds = (sp[:, None] == kinds_all[None, :]).astype(jnp.float32)
        alive = jnp.arange(pairs) < live
        return (rows[fi], rows[se], kinds, alive)

    def brick_forces(args):
        rows, fi, se, sp, vec, live = args
        xi, xj, kinds, alive = brick_inputs(rows, fi, se, sp, live)
        coupling = jnp.where(alive, pair_slope(params, xi, xj, kinds, vec), 0.0)
        sign = (fi[:, None] == columns[None, :]).astype(jnp.float32) - (se[:, None] == columns[None, :]).astype(jnp.float32)
        return jnp.dot(coupling[None, :] * vec, sign, precision=highest)
    extended = lax.map(brick_forces, (flat_table, flat_first, flat_second, flat_species, flat_vec, flat_live))
    extended = extended.reshape(nbx, nby, 3, extent)
    forces = extended[..., :atoms]
    parts = extended[..., atoms:].reshape(nbx, nby, 3, 4, ghosts)
    atom_ids = jnp.arange(atoms)
    for d, (dx, dy) in enumerate(DIRS):
        arrived = jnp.roll(parts[:, :, :, d, :], (dx, dy), axis=(0, 1))
        onehot = (send_list[:, :, d, :, None] == atom_ids).astype(jnp.float32)
        forces = forces + jnp.einsum('xycg,xyga->xyca', arrived, onehot, precision=highest)
    residual = (forces - force_target) / atoms
    residual_rows = ghost_rows(jnp.transpose(residual, (0, 1, 3, 2)), send_list)
    residual_table = jnp.concatenate([residual, jnp.transpose(residual_rows, (0, 1, 3, 2))], axis=3)
    flat_residual = residual_table.reshape(nbx * nby, 3, extent)

    def brick_grads(carry, args):
        rows, fi, se, sp, vec, live, res = args
        xi, xj, kinds, alive = brick_inputs(rows, fi, se, sp, live)
        weight = jnp.where(alive, lax.optimization_barrier(jnp.sum((res[:, fi] - res[:, se]) * vec, axis=0)), 0.0)
        _, pull = jax.vjp(lambda p: pair_slope(p, xi, xj, kinds, vec), params)
        grads = pull(weight)[0]
        return (jax.tree.map(lambda a, b: a + b, carry, grads), None)
    zero = jax.tree.map(jnp.zeros_like, params)
    grads, _ = lax.scan(brick_grads, zero, (flat_table, flat_first, flat_second, flat_species, flat_vec, flat_live, flat_residual))
    return (forces, grads[0], grads[1], grads[2], grads[3], grads[4], grads[5])
```

```python
import functools
import math

import jax
import jax.numpy as jnp
from jax import lax
from jax.experimental import pallas as pl
from jax.experimental.pallas import tpu as pltpu
from jax.sharding import Mesh
from jax.sharding import PartitionSpec as P

RCUT = 5.0
DIRS = ((1, 0), (0, 1), (1, 1), (1, -1))
AXES = ("z", "xh", "xl", "y", "c")
BX = ("z", "xh")
BY = ("xl", "y", "c")
ATOMS = 128
GHOST = 32
PAIRS = 2048
H = 512
F = 128
NB = 8
NS = 16
B = 512
STEPS = PAIRS // B
SEG = 800
HALF = 1664
f32 = jnp.float32
bf16 = jnp.bfloat16
HI = lax.Precision.HIGHEST
NT = (((1,), (1,)), ((), ()))
NN = (((1,), (0,)), ((), ()))


def split(x):
    h = x.astype(bf16)
    return h, (x - h.astype(f32)).astype(bf16)


def dot(a, b, dims=NN, precision=None):
    return lax.dot_general(a, b, dims, precision=precision, preferred_element_type=f32)


def sigmoid(x):
    return 0.5 * jnp.tanh(0.5 * x) + 0.5


def whole(shape):
    return pl.BlockSpec(shape, lambda *_: (0,) * len(shape))


def lanes(rows):
    return pl.BlockSpec((rows, B), lambda i: (0, i))


def params(mib):
    return pltpu.CompilerParams(vmem_limit_bytes=mib << 20)


def prep_kernel(feat, w_a, w_b, w_r, sp, w_m, vec, spec, w_o,
                wt_h, wt_l, w_h, w_l, tab_h, tab_l, small, wr3, wbt, ones, bsr, v8, wob):
    h, l = split(w_m[...])
    w_h[...] = h
    w_l[...] = l
    h, l = split(w_m[...].T)
    wt_h[...] = h
    wt_l[...] = l
    x = feat[...]
    h, l = split(dot(w_a[...].T, x, NT, HI))
    tab_h[:, 0:128] = h
    tab_l[:, 0:128] = l
    wb = w_b[...].T
    wbt[...] = wb
    h, l = split(dot(wb, x, NT, HI))
    tab_h[:, 128:256] = h
    tab_l[:, 128:256] = l
    wide = jnp.concatenate([sp[...], w_r[...], w_r[...], sp[...], w_r[...], jnp.zeros((72, H), f32)], 0)
    wide = wide.T
    h, l = split(wide)
    col = lax.broadcasted_iota(jnp.int32, (H, 128), 1)
    small[...] = jnp.where(col < 32, h.astype(f32), l.astype(f32)).astype(bf16)
    wide = jnp.concatenate([w_r[...], w_r[...], w_r[...], jnp.zeros((104, H), f32)], 0).T
    h, l = split(wide)
    wr3[...] = jnp.where(col < 16, h.astype(f32), l.astype(f32)).astype(bf16)
    wob[...] = jnp.broadcast_to(w_o[...], (128, H)).T
    v = vec[...]
    square = jnp.sum(v * v, axis=0, keepdims=True) + 1.0
    radius = jnp.sqrt(square)
    order = (lax.broadcasted_iota(jnp.int32, (NB, 1), 0) + 1).astype(f32) * (math.pi / RCUT)
    phase = order * radius
    sn = jnp.sin(phase)
    cs = jnp.cos(phase)
    basis = sn / radius
    slope = (order * cs / radius - sn / square) / radius
    kinds = lax.broadcasted_iota(jnp.int32, (NS, PAIRS), 0) == spec[...]
    kinds = jnp.where(kinds, 1.0, 0.0)
    bh = basis.astype(bf16).astype(f32)
    bl = basis - bh
    zero = jnp.zeros((NB, PAIRS), f32)
    ones[...] = jnp.concatenate(
        [kinds, bh, bl, kinds, bh, zero, jnp.zeros((64, PAIRS), f32)], 0).astype(bf16)
    sh = slope.astype(bf16).astype(f32)
    sl = slope - sh
    bsr[...] = jnp.concatenate([sh, sl, sh, jnp.zeros((104, PAIRS), f32)], 0).astype(bf16)
    v8[...] = jnp.concatenate([v, jnp.zeros((5, PAIRS), f32)], 0)


def prepare(feat, w_a, w_b, w_r, sp, w_m, vec, spec, w_o):
    out = lambda s, t: jax.ShapeDtypeStruct(s, t)
    return pl.pallas_call(
        prep_kernel,
        name="prep",
        out_shape=(
            out((H, H), bf16), out((H, H), bf16), out((H, H), bf16), out((H, H), bf16),
            out((H, 256), bf16), out((H, 256), bf16), out((H, 128), bf16), out((H, 128), bf16),
            out((H, F), f32), out((128, PAIRS), bf16), out((128, PAIRS), bf16), out((8, PAIRS), f32),
            out((H, 128), f32),
        ),
        compiler_params=params(24),
        cost_estimate=pl.CostEstimate(flops=3 * 10**9, bytes_accessed=8 << 20, transcendentals=0),
    )(feat, w_a, w_b, w_r, sp, w_m, vec, spec, w_o)


def onehots(fi, se):
    a = jnp.where(lax.broadcasted_iota(jnp.int32, (128, B), 0) == fi, 1.0, 0.0).astype(bf16)
    b = jnp.where(lax.broadcasted_iota(jnp.int32, (256, B), 0) == se, 1.0, 0.0).astype(bf16)
    return jnp.concatenate([a, b], 0)


def tile(x):
    return jnp.concatenate([x] * (B // 128), 1)


def forward_kernel(live, fi, se, ones, bsr, v8, g0, g1, g2, g3, tab_h, tab_l, small, wr3, wbt,
                   wt_h, wt_l, wob,
                   zh, zl, qh, ql, s1, cs2, th, mh, yy, eloc, p0, p1, p2, p3,
                   tab, acc):
    i = pl.program_id(0)

    @pl.when(i == 0)
    def _():
        tab[:, 0:256] = tab_h[...]
        tab[:, 384:640] = tab_l[...]
        ghosts = jnp.concatenate([g0[...], g1[...], g2[...], g3[...]], 0)
        h, l = split(dot(wbt[...], ghosts, NT, HI))
        tab[:, 256:384] = h
        tab[:, 640:768] = l
        tab[:, 768:896] = small[...]
        acc[...] = jnp.zeros_like(acc)

    oh = onehots(fi[...], se[...])
    pre = dot(tab[...], jnp.concatenate([oh, oh, ones[...]], 0))
    c = dot(wr3[...], bsr[...])
    for r in range(0, H, 16):
        x = pre[r:r + 16]
        cc = c[r:r + 16]
        s = sigmoid(x)
        z = x * s
        d1 = s + z * (1.0 - s)
        d2 = s * (1.0 - s) * (2.0 + x * (1.0 - 2.0 * s))
        q = d1 * cc
        s1[r:r + 16, :] = d1
        cs2[r:r + 16, :] = cc * d2
        zh[r:r + 16, :], zl[r:r + 16, :] = split(z)
        qh[r:r + 16, :], ql[r:r + 16, :] = split(q)
    w3 = jnp.concatenate([wt_h[...], wt_l[...], wt_h[...]], 1)
    m = dot(w3, jnp.concatenate([zh[...], zh[...], zl[...]], 0))
    t = dot(w3, jnp.concatenate([qh[...], qh[...], ql[...]], 0))
    total = jnp.zeros((16, B), f32)
    for r in range(0, H, 16):
        x = m[r:r + 16]
        tt = t[r:r + 16]
        w = tile(wob[r:r + 16, :])
        s = sigmoid(x)
        z = x * s
        d1 = s + z * (1.0 - s)
        d2 = s * (1.0 - s) * (2.0 + x * (1.0 - 2.0 * s))
        y = d1 * tt
        yy[r:r + 16, :] = y
        total = total + w * y
        th[r:r + 16, :] = w * d1
        mh[r:r + 16, :] = w * (d2 * tt)
    slope = jnp.sum(total, axis=0, keepdims=True)
    slot = lax.broadcasted_iota(jnp.int32, (1, B), 1) + i * B
    coupling = jnp.where(slot < live[0], slope, 0.0)
    cv = coupling * v8[...]
    ch = cv.astype(bf16).astype(f32)
    lhs = jnp.concatenate([ch, cv - ch], 0).astype(bf16)
    acc[...] += dot(lhs, oh, NT)

    @pl.when(i == STEPS - 1)
    def _():
        e = acc[0:8, :] + acc[8:16, :]
        eloc[...] = e[:, 0:128] - e[:, 128:256]
        for d, p in enumerate((p0, p1, p2, p3)):
            p[...] = -e[:, 256 + 32 * d:288 + 32 * d]


def forward(live, fi, se, ones, bsr, v8, ghosts, tab_h, tab_l, small, wr3, wbt, wt_h, wt_l, wob):
    out = lambda s, t: jax.ShapeDtypeStruct(s, t)
    big = (H, PAIRS)
    return pl.pallas_call(
        forward_kernel,
        name="forward",
        grid=(STEPS,),
        in_specs=[pl.BlockSpec(memory_space=pltpu.SMEM), lanes(1), lanes(1), lanes(128), lanes(128), lanes(8)]
        + [whole((GHOST, F))] * 4
        + [whole((H, 256)), whole((H, 256)), whole((H, 128)), whole((H, 128)), whole((H, F)),
           whole((H, H)), whole((H, H)), whole((H, 128))],
        out_specs=[lanes(H)] * 9 + [whole((8, 128))] + [whole((8, GHOST))] * 4,
        out_shape=[out(big, bf16)] * 4 + [out(big, f32)] * 5 + [out((8, 128), f32)] + [out((8, GHOST), f32)] * 4,
        scratch_shapes=[pltpu.VMEM((H, 896), bf16), pltpu.VMEM((16, 384), f32)],
        compiler_params=params(48),
        cost_estimate=pl.CostEstimate(flops=10**10, bytes_accessed=36 << 20, transcendentals=2 * H * PAIRS),
    )(live, fi, se, ones, bsr, v8, *ghosts, tab_h, tab_l, small, wr3, wbt, wt_h, wt_l, wob)


def force_kernel(eloc, r0, r1, r2, r3, sends, target, forces, residual, l0, l1, l2, l3, got):
    for d, r in enumerate((r0, r1, r2, r3)):
        got[:, 32 * d:32 * d + 32] = r[...]
    lent = jnp.where(lax.broadcasted_iota(jnp.int32, (ATOMS, 128), 0) == sends[...], 1.0, 0.0)
    total = eloc[...] + dot(got[...], lent, NT, HI)
    forces[...] = total[0:3, :]
    res = (total[0:3, :] - target[...]) / ATOMS
    res = jnp.concatenate([res, jnp.zeros((5, ATOMS), f32)], 0)
    residual[...] = res
    picked = dot(res, lent, NN, HI)
    for d, l in enumerate((l0, l1, l2, l3)):
        l[...] = picked[:, 32 * d:32 * d + 32]


def force_step(eloc, returned, sends, target):
    out = lambda s: jax.ShapeDtypeStruct(s, f32)
    return pl.pallas_call(
        force_kernel,
        name="forces",
        out_shape=[out((3, 128)), out((8, 128))] + [out((8, GHOST))] * 4,
        scratch_shapes=[pltpu.VMEM((8, 128), f32)],
        compiler_params=params(4),
    )(eloc, *returned, sends, target)


def backward_kernel(th, mh, s1, cs2, w_h, w_l, pb, cb, ah, al, bh, bl):
    for r in range(0, H, 16):
        ah[r:r + 16, :], al[r:r + 16, :] = split(mh[r:r + 16, :])
        bh[r:r + 16, :], bl[r:r + 16, :] = split(th[r:r + 16, :])
    w3 = jnp.concatenate([w_h[...], w_l[...], w_h[...]], 1)
    zb = dot(w3, jnp.concatenate([ah[...], ah[...], al[...]], 0))
    qb = dot(w3, jnp.concatenate([bh[...], bh[...], bl[...]], 0))
    for r in range(0, H, 16):
        d1 = s1[r:r + 16, :]
        q = qb[r:r + 16]
        pb[r:r + 16, :] = zb[r:r + 16] * d1 + q * cs2[r:r + 16, :]
        cb[r:r + 16, :] = q * d1


def backward(th, mh, s1, cs2, w_h, w_l, first, count):
    out = lambda s, t: jax.ShapeDtypeStruct(s, t)
    part = pl.BlockSpec((H, B), lambda i: (0, i + first))
    return pl.pallas_call(
        backward_kernel,
        name=f"backward{first}",
        grid=(count,),
        in_specs=[part] * 4 + [whole((H, H))] * 2,
        out_specs=[lanes(H)] * 2,
        out_shape=[out((H, B * count), f32)] * 2,
        scratch_shapes=[pltpu.VMEM((H, B), bf16)] * 4,
        compiler_params=params(40),
        cost_estimate=pl.CostEstimate(flops=3 * 4 * H * H * B * count, bytes_accessed=12 * H * B * count * 2, transcendentals=0),
    )(th, mh, s1, cs2, w_h, w_l)


def grad_kernel(live, core, fi, se, ones, bsr, v8, residual, g0, g1, g2, g3,
                zh, zl, qh, ql, th, mh, yy, pb0, cb0, pb1, cb1, feat, x0, x1, x2, x3,
                mine, theirs,
                table, mhh, mhl, thh, thl, ph, plo, ch, cl, wacc, gacc, racc, oacc):
    i = pl.program_id(0)

    @pl.when(i == 0)
    def _():
        def put(lo, x):
            n = x.shape[1]
            h = x.astype(bf16)
            table[0:8, lo:lo + n] = h.astype(f32)
            table[8:16, lo:lo + n] = x - h.astype(f32)
        put(0, residual[...])
        put(128, -residual[...])
        for d, g in enumerate((g0, g1, g2, g3)):
            put(256 + 32 * d, -g[...])
        wacc[...] = jnp.zeros_like(wacc)
        gacc[...] = jnp.zeros_like(gacc)
        racc[...] = jnp.zeros_like(racc)
        oacc[...] = jnp.zeros_like(oacc)

    oh = onehots(fi[...], se[...])
    gap = dot(table[...].astype(bf16), oh)
    weight = jnp.sum((gap[0:8] + gap[8:16]) * v8[...], axis=0, keepdims=True)
    slot = lax.broadcasted_iota(jnp.int32, (1, B), 1) + i * B
    weight = jnp.where(slot < live[0], weight, 0.0)
    weight = jnp.broadcast_to(weight, (16, B))
    first = i < STEPS // 2
    for r in range(0, H, 16):
        mhh[r:r + 16, :], mhl[r:r + 16, :] = split(mh[r:r + 16, :] * weight)
        thh[r:r + 16, :], thl[r:r + 16, :] = split(th[r:r + 16, :] * weight)
        pb = jnp.where(first, pb0[r:r + 16, :], pb1[r:r + 16, :])
        cb = jnp.where(first, cb0[r:r + 16, :], cb1[r:r + 16, :])
        ph[r:r + 16, :], plo[r:r + 16, :] = split(pb * weight)
        ch[r:r + 16, :], cl[r:r + 16, :] = split(cb * weight)
        y = yy[r:r + 16, :] * weight
        oacc[r:r + 16, :] += sum(y[:, k:k + 128] for k in range(0, B, 128))
    wacc[...] += dot(
        jnp.concatenate([zh[...], zh[...], zl[...], qh[...], qh[...], ql[...]], 1),
        jnp.concatenate([mhh[...], mhl[...], mhh[...], thh[...], thl[...], thh[...]], 1), NT)
    rows = jnp.concatenate([oh, ones[0:32, :]], 0)
    gacc[...] += dot(jnp.concatenate([rows, rows], 1), jnp.concatenate([ph[...], plo[...]], 1), NT)
    racc[...] += dot(
        jnp.concatenate([bsr[0:16, :], bsr[0:16, :]], 1), jnp.concatenate([ch[...], cl[...]], 1), NT)

    @pl.when(i == STEPS - 1)
    def _():
        ga = dot(feat[...].T, gacc[0:128, :], NN, HI)
        rest = jnp.concatenate([feat[...], x0[...], x1[...], x2[...], x3[...]], 0)
        gb = dot(rest.T, gacc[128:384, :], NN, HI)
        gr = gacc[400:408, :] + gacc[408:416, :] + racc[0:8, :] + racc[8:16, :]
        go = dot(jnp.ones((8, 128), f32), oacc[...], NT, HI)
        pieces = ((0, ga), (128, gb), (256, gr), (264, gacc[384:400, :]), (280, wacc[...]), (792, go))

        def write(ref, half):
            for b in range(2):
                lo = (2 * half + b) * 128
                for at, piece in pieces:
                    ref[SEG * b + at:SEG * b + at + piece.shape[0], :] = piece[:, lo:lo + 128]
            ref[2 * SEG:HALF, :] = jnp.zeros((HALF - 2 * SEG, 128), f32)

        @pl.when(core[0] == 0)
        def _():
            write(mine, 0)
            write(theirs, 1)

        @pl.when(core[0] != 0)
        def _():
            write(mine, 1)
            write(theirs, 0)


def weighted(live, core, fi, se, ones, bsr, v8, residual, g, zh, zl, qh, ql, th, mh, yy, pb0, cb0, pb1, cb1, feat, x):
    out = lambda s, t: jax.ShapeDtypeStruct(s, t)
    smem = pl.BlockSpec(memory_space=pltpu.SMEM)
    half = STEPS // 2
    lower = pl.BlockSpec((H, B), lambda i: (0, jnp.minimum(i, half - 1)))
    upper = pl.BlockSpec((H, B), lambda i: (0, jnp.maximum(i - half, 0)))
    vb = lambda: pltpu.VMEM((H, B), bf16)
    return pl.pallas_call(
        grad_kernel,
        name="weighted",
        grid=(STEPS,),
        in_specs=[smem, smem, lanes(1), lanes(1), lanes(128), lanes(128), lanes(8), whole((8, 128))]
        + [whole((8, GHOST))] * 4 + [lanes(H)] * 7 + [lower, lower, upper, upper]
        + [whole((ATOMS, F))] + [whole((GHOST, F))] * 4,
        out_specs=[whole((HALF, 128))] * 2,
        out_shape=[out((HALF, 128), f32)] * 2,
        scratch_shapes=[pltpu.VMEM((16, 384), f32)] + [vb() for _ in range(8)]
        + [pltpu.VMEM((H, H), f32), pltpu.VMEM((416, H), f32), pltpu.VMEM((16, H), f32), pltpu.VMEM((H, 128), f32)],
        compiler_params=params(52),
        cost_estimate=pl.CostEstimate(flops=10**10, bytes_accessed=36 << 20, transcendentals=0),
    )(live, core, fi, se, ones, bsr, v8, residual, *g, zh, zl, qh, ql, th, mh, yy, pb0, cb0, pb1, cb1, feat, *x)


def unpack_kernel(core, mine, other, ga, gb, gr, gs, gm, go):
    def write(ref, half):
        for b in range(2):
            lo = (2 * half + b) * 128
            for at, n, o in ((0, 128, ga), (128, 128, gb), (256, 8, gr), (264, 16, gs), (280, 512, gm), (792, 1, go)):
                o[:, lo:lo + 128] = ref[SEG * b + at:SEG * b + at + n, :]

    @pl.when(core[0] == 0)
    def _():
        write(mine, 0)
        write(other, 1)

    @pl.when(core[0] != 0)
    def _():
        write(mine, 1)
        write(other, 0)


def unpack(core, mine, other):
    out = lambda r: jax.ShapeDtypeStruct((r, H), f32)
    return pl.pallas_call(
        unpack_kernel,
        name="unpack",
        in_specs=[pl.BlockSpec(memory_space=pltpu.SMEM), whole((HALF, 128)), whole((HALF, 128))],
        out_shape=[out(128), out(128), out(8), out(16), out(512), out(1)],
        compiler_params=params(16),
    )(core, mine, other)


def moved(block, delta):
    nx, ny = (math.prod(lax.axis_size(a) for a in axes) for axes in (BX, BY))
    route = [(a * ny + b, (a + delta[0]) % nx * ny + (b + delta[1]) % ny) for a in range(nx) for b in range(ny)]
    return lax.ppermute(block, AXES, route)


def sum_over_slice(mine, theirs):
    swap = [(0, 1), (1, 0)]
    plane = ("xh", "xl", "y")
    n = math.prod(lax.axis_size(a) for a in plane)
    depth = lax.axis_size("z")
    part = (mine + lax.ppermute(theirs, "c", swap)).reshape(n, HALF // n, 128)
    part = jnp.sum(lax.all_to_all(part, plane, 0, 0, tiled=True), axis=0)
    part = part.reshape(depth, HALF // n // depth, 128)
    part = jnp.sum(lax.all_to_all(part, "z", 0, 0, tiled=True), axis=0)
    part = jnp.broadcast_to(part[None], (depth,) + part.shape)
    part = lax.all_to_all(part, "z", 0, 0, tiled=True).reshape(HALF // n, 128)
    part = jnp.broadcast_to(part[None], (n,) + part.shape)
    full = lax.all_to_all(part, plane, 0, 0, tiled=True).reshape(HALF, 128)
    return full, lax.ppermute(full, "c", swap)


def local(features, send_list, pair_first, pair_second, pair_species, pair_vector, live_pairs, force_target,
          w_a, w_b, w_radial, species_table, w_mid, w_out):
    feat = features[0, 0]
    sends = send_list[0, 0]
    fi = pair_first[0]
    se = pair_second[0]
    live = live_pairs.reshape(1)
    core = lax.axis_index("c").reshape(1)
    back = [(-dx, -dy) for dx, dy in DIRS]
    lent = jnp.take(feat, sends, axis=0)
    ghosts = [moved(lent[d], back[d]) for d in range(4)]
    (wt_h, wt_l, w_h, w_l, tab_h, tab_l, small, wr3, wbt, ones, bsr, v8, wob) = prepare(
        feat, w_a, w_b, w_radial, species_table, w_mid, pair_vector[0, 0], pair_species[0], w_out[None])
    (zh, zl, qh, ql, s1, cs2, th, mh, yy, eloc, *parts) = forward(
        live, fi, se, ones, bsr, v8, ghosts, tab_h, tab_l, small, wr3, wbt, wt_h, wt_l, wob)
    returned = [moved(parts[d], DIRS[d]) for d in range(4)]
    pb0, cb0 = backward(th, mh, s1, cs2, w_h, w_l, 0, STEPS // 2)
    forces, residual, *lent_res = force_step(eloc, returned, sends.reshape(1, 128), force_target[0, 0])
    ghost_res = [moved(lent_res[d], back[d]) for d in range(4)]
    pb1, cb1 = backward(th, mh, s1, cs2, w_h, w_l, STEPS // 2, STEPS - STEPS // 2)
    mine, theirs = weighted(live, core, fi, se, ones, bsr, v8, residual, ghost_res, zh, zl, qh, ql, th, mh, yy,
                            pb0, cb0, pb1, cb1, feat, ghosts)
    mine, other = sum_over_slice(mine, theirs)
    ga, gb, gr, gs, gm, go = unpack(core, mine, other)
    return (forces[None, None], ga, gb, gr, gs, gm, go[0])


def solution(mesh):
    inner = Mesh(mesh.devices.reshape(8, 2, 2, 4, 2), AXES)
    four = P(BX, BY, None, None)
    three = P(BX, BY, None)
    return jax.shard_map(
        local,
        mesh=inner,
        in_specs=(four, four, three, three, three, four, P(BX, BY), four, P(), P(), P(), P(), P(), P()),
        out_specs=(four, P(), P(), P(), P(), P(), P()),
        check_vma=False,
    )
```

```python
import functools
import math

import jax
import jax.numpy as jnp
from jax import lax
from jax.experimental import pallas as pl
from jax.experimental.pallas import tpu as pltpu
from jax.sharding import Mesh
from jax.sharding import PartitionSpec as P

RCUT = 5.0
DIRS = ((1, 0), (0, 1), (1, 1), (1, -1))
AXES = ("z", "xh", "xl", "y", "c")
BX = ("z", "xh")
BY = ("xl", "y", "c")
ATOMS = 128
GHOST = 32
PAIRS = 2048
H = 512
F = 128
NB = 8
NS = 16
B = 512
W = 256
STEPS = PAIRS // B
SEG = 800
HALF = 1664
f32 = jnp.float32
bf16 = jnp.bfloat16
HI = lax.Precision.HIGHEST
VMEM = 66_000_000
NT = (((1,), (1,)), ((), ()))
NN = (((1,), (0,)), ((), ()))


def split(x):
    h = x.astype(bf16)
    return h, (x - h.astype(f32)).astype(bf16)


def dot(a, b, dims=NN, precision=None):
    return lax.dot_general(a, b, dims, precision=precision, preferred_element_type=f32)


def sigmoid(x):
    return 0.5 * jnp.tanh(0.5 * x) + 0.5


def whole(shape):
    return pl.BlockSpec(shape, lambda *_: (0,) * len(shape))


def lanes(rows):
    return pl.BlockSpec((rows, B), lambda i: (0, i))


def params(limit=VMEM):
    return pltpu.CompilerParams(vmem_limit_bytes=limit)


def send_row(sends, row):
    for d in range(4):
        row[:, GHOST * d:GHOST * (d + 1)] = sends[d]
    return jnp.where(lax.broadcasted_iota(jnp.int32, (ATOMS, 128), 0) == row[...], 1.0, 0.0)


def lend_kernel(feat, sends, l0, l1, l2, l3, row):
    rows = dot(send_row(sends, row).T, feat[...], NN, HI)
    for d, l in enumerate((l0, l1, l2, l3)):
        l[...] = rows[GHOST * d:GHOST * (d + 1), :]


def lend(feat, sends):
    return pl.pallas_call(
        lend_kernel,
        name="lend",
        out_shape=[jax.ShapeDtypeStruct((GHOST, F), f32)] * 4,
        scratch_shapes=[pltpu.VMEM((1, 128), jnp.int32)],
        compiler_params=params(4 << 20),
    )(feat, sends)


def onehots(fi, se):
    n = fi.shape[1]
    a = jnp.where(lax.broadcasted_iota(jnp.int32, (128, n), 0) == fi, 1.0, 0.0).astype(bf16)
    b = jnp.where(lax.broadcasted_iota(jnp.int32, (256, n), 0) == se, 1.0, 0.0).astype(bf16)
    return jnp.concatenate([a, b], 0)


def species_hot(sp):
    return jnp.where(lax.broadcasted_iota(jnp.int32, (NS, sp.shape[1]), 0) == sp, 1.0, 0.0)


def parts_of(x):
    h = x.astype(bf16).astype(f32)
    return h, x - h


def tile(x, n):
    return jnp.concatenate([x] * (n // 128), 1)


def forward_kernel(live, fi, se, sp, vec, feat, g0, g1, g2, g3, w_a, w_b, w_r, w_s, w_m, w_o,
                   zh, zl, qh, ql, s1, cs2, th, mh, yy, basis, slopes, eloc, p0, p1, p2, p3,
                   tab, wt, wr3, wob, acc):
    i = pl.program_id(0)

    @pl.when(i == 0)
    def _():
        wt[:, 0:H], wt[:, H:2 * H] = split(w_m[...].T)
        table = jnp.concatenate([feat[...], g0[...], g1[...], g2[...], g3[...]], 0)
        tab[:, 0:128], tab[:, 384:512] = split(dot(w_a[...].T, feat[...], NT, HI))
        tab[:, 128:384], tab[:, 512:768] = split(dot(w_b[...].T, table, NT, HI))
        ws, wr = w_s[...], w_r[...]
        wide = jnp.concatenate([ws, wr, wr, ws, wr, jnp.zeros((72, H), f32)], 0).T
        h, l = parts_of(wide)
        col = lax.broadcasted_iota(jnp.int32, (H, 128), 1)
        tab[:, 768:896] = jnp.where(col < 32, h, l).astype(bf16)
        h, l = parts_of(jnp.concatenate([wr, wr, wr, jnp.zeros((104, H), f32)], 0).T)
        wr3[...] = jnp.where(col < 16, h, l).astype(bf16)
        wob[...] = jnp.broadcast_to(w_o[...], (128, H)).T
        acc[...] = jnp.zeros_like(acc)

    v = jnp.concatenate([vec[0], vec[1], vec[2]], 0)
    square = jnp.sum(v * v, axis=0, keepdims=True) + 1.0
    radius = jnp.sqrt(square)
    order = (lax.broadcasted_iota(jnp.int32, (NB, 1), 0) + 1).astype(f32) * (math.pi / RCUT)
    phase = order * radius
    sn = jnp.sin(phase)
    cs = jnp.cos(phase)
    base = sn / radius
    rate = (order * cs / radius - sn / square) / radius
    basis[...] = base
    slopes[...] = rate
    kinds = species_hot(sp[...])
    bh, bl = parts_of(base)
    ones = jnp.concatenate([kinds, bh, bl, kinds, bh, jnp.zeros((72, B), f32)], 0).astype(bf16)
    sh, sl = parts_of(rate)
    bsr = jnp.concatenate([sh, sl, sh, jnp.zeros((104, B), f32)], 0).astype(bf16)
    v8 = jnp.concatenate([v, jnp.zeros((5, B), f32)], 0)
    oh = onehots(fi[...], se[...])
    w3 = jnp.concatenate([wt[...], wt[:, 0:H]], 1)
    spans = [slice(lo, lo + W) for lo in range(0, B, W)]

    def enter(k):
        pre = dot(tab[...], jnp.concatenate([oh[:, k], oh[:, k], ones[:, k]], 0))
        return pre, dot(wr3[...], bsr[:, k])

    def first(k, pre, c):
        for r in range(0, H, 16):
            x = pre[r:r + 16]
            cc = c[r:r + 16]
            s = sigmoid(x)
            z = x * s
            n = 1.0 - s
            d1 = s + z * n
            d2 = s * n * (2.0 + x * (n - s))
            q = d1 * cc
            s1[r:r + 16, k] = d1
            cs2[r:r + 16, k] = cc * d2
            zh[r:r + 16, k], zl[r:r + 16, k] = split(z)
            qh[r:r + 16, k], ql[r:r + 16, k] = split(q)

    def middle(k):
        m = dot(w3, jnp.concatenate([zh[:, k], zh[:, k], zl[:, k]], 0))
        return m, dot(w3, jnp.concatenate([qh[:, k], qh[:, k], ql[:, k]], 0))

    def last(k, m, t):
        total = jnp.zeros((16, W), f32)
        for r in range(0, H, 16):
            x = m[r:r + 16]
            tt = t[r:r + 16]
            w = tile(wob[r:r + 16, :], W)
            s = sigmoid(x)
            z = x * s
            n = 1.0 - s
            d1 = s + z * n
            d2 = s * n * (2.0 + x * (n - s))
            y = d1 * tt
            yy[r:r + 16, k] = y
            total = total + w * y
            th[r:r + 16, k] = w * d1
            mh[r:r + 16, k] = w * (d2 * tt)
        return jnp.sum(total, axis=0, keepdims=True)

    pres = [enter(k) for k in spans]
    mids = []
    for k, (pre, c) in zip(spans, pres):
        first(k, pre, c)
        mids.append(middle(k))
    slope = jnp.concatenate([last(k, m, t) for k, (m, t) in zip(spans, mids)], 1)
    slot = lax.broadcasted_iota(jnp.int32, (1, B), 1) + i * B
    coupling = jnp.where(slot < live[0], slope, 0.0)
    lhs = jnp.concatenate(parts_of(coupling * v8), 0).astype(bf16)
    acc[...] += dot(lhs, oh, NT)

    @pl.when(i == STEPS - 1)
    def _():
        e = acc[0:8, :] + acc[8:16, :]
        eloc[...] = e[:, 0:128] - e[:, 128:256]
        for d, p in enumerate((p0, p1, p2, p3)):
            p[...] = -e[:, 256 + 32 * d:288 + 32 * d]


VEC = pl.BlockSpec((3, 1, B), lambda i: (0, 0, i))
WEIGHTS = [whole((F, H)), whole((F, H)), whole((NB, H)), whole((NS, H)), whole((H, H)), whole((1, H))]


def forward(live, fi, se, sp, vec, feat, ghosts, weights):
    out = lambda s, t: jax.ShapeDtypeStruct(s, t)
    big = (H, PAIRS)
    return pl.pallas_call(
        forward_kernel,
        name="forward",
        grid=(STEPS,),
        in_specs=[pl.BlockSpec(memory_space=pltpu.SMEM), lanes(1), lanes(1), lanes(1), VEC, whole((ATOMS, F))]
        + [whole((GHOST, F))] * 4 + WEIGHTS,
        out_specs=[lanes(H)] * 9 + [lanes(NB)] * 2 + [whole((8, 128))] + [whole((8, GHOST))] * 4,
        out_shape=[out(big, bf16)] * 4 + [out(big, f32)] * 5 + [out((NB, PAIRS), f32)] * 2
        + [out((8, 128), f32)] + [out((8, GHOST), f32)] * 4,
        scratch_shapes=[pltpu.VMEM((H, 896), bf16), pltpu.VMEM((H, 2 * H), bf16), pltpu.VMEM((H, 128), bf16),
                        pltpu.VMEM((H, 128), f32), pltpu.VMEM((16, 384), f32)],
        compiler_params=params(),
        cost_estimate=pl.CostEstimate(flops=10**10, bytes_accessed=36 << 20, transcendentals=2 * H * PAIRS),
    )(live, fi, se, sp, vec, feat, *ghosts, *weights)


def force_kernel(eloc, r0, r1, r2, r3, sends, target, forces, residual, l0, l1, l2, l3, got, row):
    for d, r in enumerate((r0, r1, r2, r3)):
        got[:, GHOST * d:GHOST * (d + 1)] = r[...]
    lent = send_row(sends, row)
    total = eloc[...] + dot(got[...], lent, NT, HI)
    goal = jnp.concatenate([target[0], target[1], target[2]], 0)
    for k in range(3):
        forces[k] = total[k:k + 1, :]
    res = (total[0:3, :] - goal) / ATOMS
    res = jnp.concatenate([res, jnp.zeros((5, ATOMS), f32)], 0)
    residual[...] = res
    picked = dot(res, lent, NN, HI)
    for d, l in enumerate((l0, l1, l2, l3)):
        l[...] = picked[:, GHOST * d:GHOST * (d + 1)]


def force_step(eloc, returned, sends, target):
    out = lambda s: jax.ShapeDtypeStruct(s, f32)
    return pl.pallas_call(
        force_kernel,
        name="forces",
        out_shape=[out((3, 1, 128)), out((8, 128))] + [out((8, GHOST))] * 4,
        scratch_shapes=[pltpu.VMEM((8, 128), f32), pltpu.VMEM((1, 128), jnp.int32)],
        compiler_params=params(4 << 20),
    )(eloc, *returned, sends, target)


def grad_kernel(live, core, fi, se, sp, vec, basis, slopes, residual, g0, g1, g2, g3,
                zh, zl, qh, ql, th, mh, yy, s1, cs2, w_m, feat, x0, x1, x2, x3,
                mine, theirs,
                table, ww, ah, al, bh, bl, ph, plo, ch, cl, wacc, gacc, racc, oacc):
    i = pl.program_id(0)

    @pl.when(i == 0)
    def _():
        def put(lo, x):
            h, l = parts_of(x)
            table[0:8, lo:lo + x.shape[1]] = h
            table[8:16, lo:lo + x.shape[1]] = l
        put(0, residual[...])
        put(128, -residual[...])
        for d, g in enumerate((g0, g1, g2, g3)):
            put(256 + GHOST * d, -g[...])
        ww[:, 0:H], ww[:, H:2 * H] = split(w_m[...])
        wacc[...] = jnp.zeros_like(wacc)
        gacc[...] = jnp.zeros_like(gacc)
        racc[...] = jnp.zeros_like(racc)
        oacc[...] = jnp.zeros_like(oacc)

    oh = onehots(fi[...], se[...])
    gap = dot(table[...].astype(bf16), oh)
    gap = gap[0:8] + gap[8:16]
    weight = gap[0:1] * vec[0] + gap[1:2] * vec[1] + gap[2:3] * vec[2]
    slot = lax.broadcasted_iota(jnp.int32, (1, B), 1) + i * B
    weight = jnp.broadcast_to(jnp.where(slot < live[0], weight, 0.0), (16, B))
    w3 = jnp.concatenate([ww[...], ww[:, 0:H]], 1)
    for r in range(0, H, 16):
        ah[r:r + 16, :], al[r:r + 16, :] = split(mh[r:r + 16, :] * weight)
        bh[r:r + 16, :], bl[r:r + 16, :] = split(th[r:r + 16, :] * weight)
        y = yy[r:r + 16, :] * weight
        oacc[r:r + 16, :] += sum(y[:, k:k + 128] for k in range(0, B, 128))
    zb = dot(w3, jnp.concatenate([ah[...], ah[...], al[...]], 0))
    qb = dot(w3, jnp.concatenate([bh[...], bh[...], bl[...]], 0))
    wacc[...] += dot(
        jnp.concatenate([zh[...], zh[...], zl[...], qh[...], qh[...], ql[...]], 1),
        jnp.concatenate([ah[...], al[...], ah[...], bh[...], bl[...], bh[...]], 1), NT)
    for r in range(0, H, 16):
        d1 = s1[r:r + 16, :]
        q = qb[r:r + 16]
        ph[r:r + 16, :], plo[r:r + 16, :] = split(zb[r:r + 16] * d1 + q * cs2[r:r + 16, :])
        ch[r:r + 16, :], cl[r:r + 16, :] = split(q * d1)
    rows = jnp.concatenate(
        [oh, jnp.concatenate([species_hot(sp[...]), *parts_of(basis[...])], 0).astype(bf16)], 0)
    gacc[...] += dot(jnp.concatenate([rows, rows], 1), jnp.concatenate([ph[...], plo[...]], 1), NT)
    rates = jnp.concatenate(parts_of(slopes[...]), 0).astype(bf16)
    racc[...] += dot(jnp.concatenate([rates, rates], 1), jnp.concatenate([ch[...], cl[...]], 1), NT)

    @pl.when(i == STEPS - 1)
    def _():
        ga = dot(feat[...].T, gacc[0:128, :], NN, HI)
        rest = jnp.concatenate([feat[...], x0[...], x1[...], x2[...], x3[...]], 0)
        gb = dot(rest.T, gacc[128:384, :], NN, HI)
        gr = gacc[400:408, :] + gacc[408:416, :] + racc[0:8, :] + racc[8:16, :]
        go = dot(jnp.ones((8, 128), f32), oacc[...], NT, HI)
        pieces = ((0, ga), (128, gb), (256, gr), (264, gacc[384:400, :]), (280, wacc[...]), (792, go))

        def write(ref, half):
            for b in range(2):
                lo = (2 * half + b) * 128
                for at, piece in pieces:
                    ref[SEG * b + at:SEG * b + at + piece.shape[0], :] = piece[:, lo:lo + 128]
            ref[2 * SEG:HALF, :] = jnp.zeros((HALF - 2 * SEG, 128), f32)

        @pl.when(core[0] == 0)
        def _():
            write(mine, 0)
            write(theirs, 1)

        @pl.when(core[0] != 0)
        def _():
            write(mine, 1)
            write(theirs, 0)


def weighted(live, core, fi, se, sp, vec, basis, slopes, residual, g, zh, zl, qh, ql, th, mh, yy, s1, cs2, w_m, feat, x):
    out = lambda s, t: jax.ShapeDtypeStruct(s, t)
    smem = pl.BlockSpec(memory_space=pltpu.SMEM)
    return pl.pallas_call(
        grad_kernel,
        name="weighted",
        grid=(STEPS,),
        in_specs=[smem, smem, lanes(1), lanes(1), lanes(1), VEC, lanes(NB), lanes(NB), whole((8, 128))]
        + [whole((8, GHOST))] * 4 + [lanes(H)] * 9
        + [whole((H, H)), whole((ATOMS, F))] + [whole((GHOST, F))] * 4,
        out_specs=[whole((HALF, 128))] * 2,
        out_shape=[out((HALF, 128), f32)] * 2,
        scratch_shapes=[pltpu.VMEM((16, 384), f32), pltpu.VMEM((H, 2 * H), bf16)]
        + [pltpu.VMEM((H, B), bf16) for _ in range(8)]
        + [pltpu.VMEM((H, H), f32), pltpu.VMEM((416, H), f32), pltpu.VMEM((16, H), f32), pltpu.VMEM((H, 128), f32)],
        compiler_params=params(),
        cost_estimate=pl.CostEstimate(flops=10**10, bytes_accessed=36 << 20, transcendentals=0),
    )(live, core, fi, se, sp, vec, basis, slopes, residual, *g, zh, zl, qh, ql, th, mh, yy, s1, cs2, w_m, feat, *x)


def unpack_kernel(core, mine, other, ga, gb, gr, gs, gm, go):
    def write(ref, half):
        for b in range(2):
            lo = (2 * half + b) * 128
            for at, n, o in ((0, 128, ga), (128, 128, gb), (256, 8, gr), (264, 16, gs), (280, 512, gm), (792, 1, go)):
                o[:, lo:lo + 128] = ref[SEG * b + at:SEG * b + at + n, :]

    @pl.when(core[0] == 0)
    def _():
        write(mine, 0)
        write(other, 1)

    @pl.when(core[0] != 0)
    def _():
        write(mine, 1)
        write(other, 0)


def unpack(core, mine, other):
    out = lambda r: jax.ShapeDtypeStruct((r, H), f32)
    return pl.pallas_call(
        unpack_kernel,
        name="unpack",
        in_specs=[pl.BlockSpec(memory_space=pltpu.SMEM), whole((HALF, 128)), whole((HALF, 128))],
        out_shape=[out(128), out(128), out(8), out(16), out(512), out(1)],
        compiler_params=params(),
    )(core, mine, other)


def moved(block, delta):
    nx, ny = (math.prod(lax.axis_size(a) for a in axes) for axes in (BX, BY))
    route = [(a * ny + b, (a + delta[0]) % nx * ny + (b + delta[1]) % ny) for a in range(nx) for b in range(ny)]
    return lax.ppermute(block, AXES, route)


def sum_over_slice(mine, theirs):
    swap = [(0, 1), (1, 0)]
    plane = ("xh", "xl", "y")
    n = math.prod(lax.axis_size(a) for a in plane)
    depth = lax.axis_size("z")
    part = (mine + lax.ppermute(theirs, "c", swap)).reshape(n, HALF // n, 128)
    part = jnp.sum(lax.all_to_all(part, plane, 0, 0, tiled=True), axis=0)
    part = jnp.broadcast_to(part[None], (depth,) + part.shape)
    part = jnp.sum(lax.all_to_all(part, "z", 0, 0, tiled=True), axis=0)
    part = jnp.broadcast_to(part[None], (n,) + part.shape)
    full = lax.all_to_all(part, plane, 0, 0, tiled=True).reshape(HALF, 128)
    return full, lax.ppermute(full, "c", swap)


def local(features, send_list, pair_first, pair_second, pair_species, pair_vector, live_pairs, force_target,
          w_a, w_b, w_radial, species_table, w_mid, w_out):
    feat = features[0, 0]
    sends = send_list.reshape(4, 1, GHOST)
    fi = pair_first[0]
    se = pair_second[0]
    sp = pair_species[0]
    vec = pair_vector.reshape(3, 1, PAIRS)
    live = live_pairs.reshape(1)
    core = lax.axis_index("c").reshape(1)
    weights = (w_a, w_b, w_radial, species_table, w_mid, w_out[None])
    back = [(-dx, -dy) for dx, dy in DIRS]
    lent = lend(feat, sends)
    ghosts = [moved(lent[d], back[d]) for d in range(4)]
    (zh, zl, qh, ql, s1, cs2, th, mh, yy, basis, slopes, eloc, *parts) = forward(
        live, fi, se, sp, vec, feat, ghosts, weights)
    returned = [moved(parts[d], DIRS[d]) for d in range(4)]
    forces, residual, *lent_res = force_step(eloc, returned, sends, force_target.reshape(3, 1, ATOMS))
    ghost_res = [moved(lent_res[d], back[d]) for d in range(4)]
    mine, theirs = weighted(live, core, fi, se, sp, vec, basis, slopes, residual, ghost_res,
                            zh, zl, qh, ql, th, mh, yy, s1, cs2, w_mid, feat, ghosts)
    mine, other = sum_over_slice(mine, theirs)
    ga, gb, gr, gs, gm, go = unpack(core, mine, other)
    return (forces.reshape(1, 1, 3, ATOMS), ga, gb, gr, gs, gm, go[0])


def solution(mesh):
    inner = Mesh(mesh.devices.reshape(8, 2, 2, 4, 2), AXES)
    four = P(BX, BY, None, None)
    three = P(BX, BY, None)
    return jax.shard_map(
        local,
        mesh=inner,
        in_specs=(four, four, three, three, three, four, P(BX, BY), four, P(), P(), P(), P(), P(), P()),
        out_specs=(four, P(), P(), P(), P(), P(), P()),
        check_vma=False,
    )
```

```python
import functools
import math

import jax
import jax.numpy as jnp
from jax import lax
from jax.experimental import pallas as pl
from jax.experimental.pallas import tpu as pltpu
from jax.sharding import Mesh
from jax.sharding import PartitionSpec as P

RCUT = 5.0
AXES = ("zh", "zl", "xh", "xl", "y", "c")
BX = ("zh", "zl", "xh")
BY = ("xl", "y", "c")
ATOMS = 128
GHOST = 32
PAIRS = 2048
H = 512
F = 128
NB = 8
NS = 16
B = 512
W = 256
BG = 512
WG = 256
SEG = 800
HALF = 1792
STEPS = PAIRS // B
STEPSG = PAIRS // BG
f32 = jnp.float32
bf16 = jnp.bfloat16
HI = lax.Precision.HIGHEST
VMEM = 64_000_000
FWD = VMEM
GRAD = 56 << 20
NT = (((1,), (1,)), ((), ()))
NN = (((1,), (0,)), ((), ()))


def split(x):
    h = x.astype(bf16)
    return h, (x - h.astype(f32)).astype(bf16)


def dot(a, b, dims=NN, precision=None):
    return lax.dot_general(a, b, dims, precision=precision, preferred_element_type=f32)


def sigmoid(x):
    return 0.5 * jnp.tanh(0.5 * x) + 0.5


def whole(shape):
    return pl.BlockSpec(shape, lambda *_: (0,) * len(shape))


def lanes(rows):
    return pl.BlockSpec((rows, B), lambda i: (0, i))


def glanes(rows):
    return pl.BlockSpec((rows, BG), lambda i: (0, i))


def params(limit=VMEM):
    return pltpu.CompilerParams(vmem_limit_bytes=limit)


def send_row(sends, row):
    for d in range(4):
        row[:, GHOST * d:GHOST * (d + 1)] = sends[d]
    return jnp.where(lax.broadcasted_iota(jnp.int32, (ATOMS, 128), 0) == row[...], 1.0, 0.0)


def lend_kernel(feat, sends, l0, l1, l2, l3, row):
    rows = dot(send_row(sends, row).T, feat[...], NN, HI)
    rows = [rows[GHOST * d:GHOST * (d + 1), :] for d in range(4)]
    for d, l in enumerate((l0, l1, l2, l3)):
        l[...] = rows[d]


def lend(feat, sends):
    return pl.pallas_call(
        lend_kernel,
        name="lend",
        out_shape=[jax.ShapeDtypeStruct((GHOST, F), f32)] * 4,
        scratch_shapes=[pltpu.VMEM((1, 128), jnp.int32)],
        compiler_params=params(),
    )(feat, sends)


def onehots(fi, se):
    n = fi.shape[1]
    a = jnp.where(lax.broadcasted_iota(jnp.int32, (128, n), 0) == fi, 1.0, 0.0).astype(bf16)
    b = jnp.where(lax.broadcasted_iota(jnp.int32, (256, n), 0) == se, 1.0, 0.0).astype(bf16)
    return jnp.concatenate([a, b], 0)


def species_hot(sp):
    return jnp.where(lax.broadcasted_iota(jnp.int32, (NS, sp.shape[1]), 0) == sp, 1.0, 0.0)


def parts_of(x):
    h = x.astype(bf16).astype(f32)
    return h, x - h


def tile(x, n):
    return jnp.concatenate([x] * (n // 128), 1)


def forward_kernel(live, fi, se, sp, vec, feat, gx, g1, g2, g3, w_a, w_b, w_r, w_s, w_m, w_o,
                   zh, zl, qh, ql, pre_out, c_out, m_out, t_out, basis, slopes, eloc, p0, p1, p2, p3,
                   tab, wt, wr3, wob, acc):
    i = pl.program_id(0)

    @pl.when(i == 0)
    def _():
        wt[:, 0:H], wt[:, H:2 * H] = split(w_m[...].T)
        table = jnp.concatenate([feat[...], gx[...], g1[...], g2[...], g3[...]], 0)
        tab[:, 0:128], tab[:, 384:512] = split(dot(w_a[...].T, feat[...], NT, HI))
        tab[:, 128:384], tab[:, 512:768] = split(dot(w_b[...].T, table, NT, HI))
        ws, wr = w_s[...], w_r[...]
        wide = jnp.concatenate([ws, wr, wr, ws, wr, jnp.zeros((72, H), f32)], 0).T
        h, l = parts_of(wide)
        col = lax.broadcasted_iota(jnp.int32, (H, 128), 1)
        tab[:, 768:896] = jnp.where(col < 32, h, l).astype(bf16)
        h, l = parts_of(jnp.concatenate([wr, wr, wr, jnp.zeros((104, H), f32)], 0).T)
        wr3[...] = jnp.where(col < 16, h, l).astype(bf16)
        wob[...] = jnp.broadcast_to(w_o[...], (128, H)).T
        acc[...] = jnp.zeros_like(acc)

    v = jnp.concatenate([vec[0], vec[1], vec[2]], 0)
    square = jnp.sum(v * v, axis=0, keepdims=True) + 1.0
    radius = jnp.sqrt(square)
    order = (lax.broadcasted_iota(jnp.int32, (NB, 1), 0) + 1).astype(f32) * (math.pi / RCUT)
    phase = order * radius
    sn = jnp.sin(phase)
    cs = jnp.cos(phase)
    base = sn / radius
    rate = (order * cs / radius - sn / square) / radius
    basis[...] = base
    slopes[...] = rate
    kinds = species_hot(sp[...])
    bh, bl = parts_of(base)
    ones = jnp.concatenate([kinds, bh, bl, kinds, bh, jnp.zeros((72, B), f32)], 0).astype(bf16)
    sh, sl = parts_of(rate)
    bsr = jnp.concatenate([sh, sl, sh, jnp.zeros((104, B), f32)], 0).astype(bf16)
    v8 = jnp.concatenate([v, jnp.zeros((5, B), f32)], 0)
    oh = onehots(fi[...], se[...])
    w3 = jnp.concatenate([wt[...], wt[:, 0:H]], 1)
    spans = [slice(lo, lo + W) for lo in range(0, B, W)]

    def enter(k):
        pre = dot(tab[...], jnp.concatenate([oh[:, k], oh[:, k], ones[:, k]], 0))
        return pre, dot(wr3[...], bsr[:, k])

    def first(k, pre, c):
        for r in range(0, H, 16):
            x = pre[r:r + 16]
            cc = c[r:r + 16]
            s = sigmoid(x)
            z = x * s
            pre_out[r:r + 16, k] = x
            c_out[r:r + 16, k] = cc
            zh[r:r + 16, k], zl[r:r + 16, k] = split(z)
            qh[r:r + 16, k], ql[r:r + 16, k] = split((s + z * (1.0 - s)) * cc)

    def middle(k):
        m = dot(w3, jnp.concatenate([zh[:, k], zh[:, k], zl[:, k]], 0))
        return m, dot(w3, jnp.concatenate([qh[:, k], qh[:, k], ql[:, k]], 0))

    def last(k, m, t):
        total = jnp.zeros((16, W), f32)
        for r in range(0, H, 16):
            x = m[r:r + 16]
            tt = t[r:r + 16]
            s = sigmoid(x)
            z = x * s
            m_out[r:r + 16, k] = x
            t_out[r:r + 16, k] = tt
            total = total + tile(wob[r:r + 16, :], W) * ((s + z * (1.0 - s)) * tt)
        return jnp.sum(total, axis=0, keepdims=True)

    pres = [enter(k) for k in spans]
    mids = []
    for k, (pre, c) in zip(spans, pres):
        first(k, pre, c)
        mids.append(middle(k))
    slope = jnp.concatenate([last(k, m, t) for k, (m, t) in zip(spans, mids)], 1)
    slot = lax.broadcasted_iota(jnp.int32, (1, B), 1) + i * B
    coupling = jnp.where(slot < live[0], slope, 0.0)
    lhs = jnp.concatenate(parts_of(coupling * v8), 0).astype(bf16)
    acc[...] += dot(lhs, oh, NT)

    @pl.when(i == STEPS - 1)
    def _():
        e = acc[0:8, :] + acc[8:16, :]
        eloc[...] = e[:, 0:128] - e[:, 128:256]
        parts = [-e[:, 256 + 32 * d:288 + 32 * d] for d in range(4)]
        for d, p in enumerate((p0, p1, p2, p3)):
            p[...] = parts[d]


VEC = pl.BlockSpec((3, 1, B), lambda i: (0, 0, i))
GVEC = pl.BlockSpec((3, 1, BG), lambda i: (0, 0, i))
WEIGHTS = [whole((F, H)), whole((F, H)), whole((NB, H)), whole((NS, H)), whole((H, H)), whole((1, H))]


def forward(live, fi, se, sp, vec, feat, ghosts, weights):
    out = lambda s, t: jax.ShapeDtypeStruct(s, t)
    big = (H, PAIRS)
    return pl.pallas_call(
        forward_kernel,
        name="forward",
        grid=(STEPS,),
        in_specs=[pl.BlockSpec(memory_space=pltpu.SMEM), lanes(1), lanes(1), lanes(1), VEC, whole((ATOMS, F))]
        + [whole((GHOST, F))] * 4 + WEIGHTS,
        out_specs=[lanes(H)] * 8 + [lanes(NB)] * 2 + [whole((8, 128))] + [whole((8, GHOST))] * 4,
        out_shape=[out(big, bf16)] * 4 + [out(big, f32)] * 4 + [out((NB, PAIRS), f32)] * 2
        + [pltpu.VMEM((8, 128), f32)] + [out((8, GHOST), f32)] * 4,
        scratch_shapes=[pltpu.VMEM((H, 896), bf16), pltpu.VMEM((H, 2 * H), bf16), pltpu.VMEM((H, 128), bf16),
                        pltpu.VMEM((H, 128), f32), pltpu.VMEM((16, 384), f32)],
        compiler_params=params(FWD),
        cost_estimate=pl.CostEstimate(flops=10**10, bytes_accessed=36 << 20, transcendentals=2 * H * PAIRS),
    )(live, fi, se, sp, vec, feat, *ghosts, *weights)


def force_kernel(eloc, rx, r1, r2, r3, sends, target, forces, residual, l0, l1, l2, l3, got, row):
    for d, r in enumerate((rx[...], r1[...], r2[...], r3[...])):
        got[:, GHOST * d:GHOST * (d + 1)] = r
    lent = send_row(sends, row)
    total = eloc[...] + dot(got[...], lent, NT, HI)
    goal = jnp.concatenate([target[0], target[1], target[2]], 0)
    for k in range(3):
        forces[k] = total[k:k + 1, :]
    res = (total[0:3, :] - goal) / ATOMS
    res = jnp.concatenate([res, jnp.zeros((5, ATOMS), f32)], 0)
    residual[...] = res
    picked = dot(res, lent, NN, HI)
    picked = [picked[:, GHOST * d:GHOST * (d + 1)] for d in range(4)]
    for d, l in enumerate((l0, l1, l2, l3)):
        l[...] = picked[d]


def force_step(eloc, returned, sends, target):
    out = lambda s: jax.ShapeDtypeStruct(s, f32)
    return pl.pallas_call(
        force_kernel,
        name="forces",
        out_shape=[out((3, 1, 128)), pltpu.HBM((8, 128), f32)] + [out((8, GHOST))] * 4,
        scratch_shapes=[pltpu.VMEM((8, 128), f32), pltpu.VMEM((1, 128), jnp.int32)],
        compiler_params=params(4 << 20),
    )(eloc, *returned, sends, target)


def grad_kernel(live, core, fi, se, sp, vec, basis, slopes, residual, gx, g1, g2, g3,
                zh, zl, qh, ql, pre, c, m_in, t_in, w_m, w_o, feat, xx, x1, x2, x3,
                mine, theirs,
                table, ww, wob, ah, al, bh, bl, ph, plo, ch, cl, wacc, gacc, racc, oacc):
    i = pl.program_id(0)

    @pl.when(i == 0)
    def _():
        def put(lo, x):
            h, l = parts_of(x)
            table[0:8, lo:lo + x.shape[1]] = h
            table[8:16, lo:lo + x.shape[1]] = l
        put(0, residual[...])
        put(128, -residual[...])
        for d, g in enumerate((gx[...], g1[...], g2[...], g3[...])):
            put(256 + GHOST * d, -g)
        ww[:, 0:H], ww[:, H:2 * H] = split(w_m[...])
        wob[...] = jnp.broadcast_to(w_o[...], (128, H)).T
        wacc[...] = jnp.zeros_like(wacc)
        gacc[...] = jnp.zeros_like(gacc)
        racc[...] = jnp.zeros_like(racc)
        oacc[...] = jnp.zeros_like(oacc)

    oh = onehots(fi[...], se[...])
    gap = dot(table[...].astype(bf16), oh)
    gap = gap[0:8] + gap[8:16]
    weight = gap[0:1] * vec[0] + gap[1:2] * vec[1] + gap[2:3] * vec[2]
    slot = lax.broadcasted_iota(jnp.int32, (1, BG), 1) + i * BG
    weight = jnp.broadcast_to(jnp.where(slot < live[0], weight, 0.0), (16, BG))
    w3 = jnp.concatenate([ww[...], ww[:, 0:H]], 1)
    rows = jnp.concatenate(
        [oh, jnp.concatenate([species_hot(sp[...]), *parts_of(basis[...])], 0).astype(bf16)], 0)
    rates = jnp.concatenate(parts_of(slopes[...]), 0).astype(bf16)

    def enter(k):
        wk = weight[:, k]
        for r in range(0, H, 16):
            x = m_in[r:r + 16, k]
            tt = t_in[r:r + 16, k]
            w = tile(wob[r:r + 16, :], WG)
            s = sigmoid(x)
            n = 1.0 - s
            d1 = (s + x * s * n) * wk
            d2 = s * n * (2.0 + x * (n - s)) * tt
            ah[r:r + 16, k], al[r:r + 16, k] = split(w * (d2 * wk))
            bh[r:r + 16, k], bl[r:r + 16, k] = split(w * d1)
            y = d1 * tt
            oacc[r:r + 16, :] += sum(y[:, j:j + 128] for j in range(0, WG, 128))

    def back(k):
        return (dot(w3, jnp.concatenate([ah[:, k], ah[:, k], al[:, k]], 0)),
                dot(w3, jnp.concatenate([bh[:, k], bh[:, k], bl[:, k]], 0)))

    def outer(k):
        wacc[...] += dot(
            jnp.concatenate([zh[:, k], zh[:, k], zl[:, k], qh[:, k], qh[:, k], ql[:, k]], 1),
            jnp.concatenate([ah[:, k], al[:, k], ah[:, k], bh[:, k], bl[:, k], bh[:, k]], 1), NT)

    def leave(k, zb, qb):
        for r in range(0, H, 16):
            x = pre[r:r + 16, k]
            s = sigmoid(x)
            n = 1.0 - s
            d1 = s + x * s * n
            d2 = s * n * (2.0 + x * (n - s))
            q = qb[r:r + 16]
            ph[r:r + 16, k], plo[r:r + 16, k] = split(zb[r:r + 16] * d1 + q * (c[r:r + 16, k] * d2))
            ch[r:r + 16, k], cl[r:r + 16, k] = split(q * d1)

    def sums(k):
        gacc[...] += dot(jnp.concatenate([rows[:, k], rows[:, k]], 1),
                         jnp.concatenate([ph[:, k], plo[:, k]], 1), NT)
        racc[...] += dot(jnp.concatenate([rates[:, k], rates[:, k]], 1),
                         jnp.concatenate([ch[:, k], cl[:, k]], 1), NT)

    spans = [slice(lo, lo + WG) for lo in range(0, BG, WG)]
    enter(spans[0])
    for n, k in enumerate(spans):
        got = back(k)
        if n + 1 < len(spans):
            enter(spans[n + 1])
        if n:
            sums(spans[n - 1])
        outer(k)
        leave(k, *got)
    sums(spans[-1])

    @pl.when(i == STEPSG - 1)
    def _():
        ga = dot(feat[...].T, gacc[0:128, :], NN, HI)
        rest = jnp.concatenate([feat[...], xx[...], x1[...], x2[...], x3[...]], 0)
        gb = dot(rest.T, gacc[128:384, :], NN, HI)
        gr = gacc[400:408, :] + gacc[408:416, :] + racc[0:8, :] + racc[8:16, :]
        go = dot(jnp.ones((8, 128), f32), oacc[...], NT, HI)
        pieces = ((0, ga), (128, gb), (256, gr), (264, gacc[384:400, :]), (280, wacc[...]), (792, go))

        def write(ref, half):
            for b in range(2):
                at0 = (2 * half + b) * 128
                for at, piece in pieces:
                    ref[SEG * b + at:SEG * b + at + piece.shape[0], :] = piece[:, at0:at0 + 128]
            ref[2 * SEG:HALF, :] = jnp.zeros((HALF - 2 * SEG, 128), f32)

        @pl.when(core[0] == 0)
        def _():
            write(mine, 0)
            write(theirs, 1)

        @pl.when(core[0] != 0)
        def _():
            write(mine, 1)
            write(theirs, 0)


def weighted(live, core, fi, se, sp, vec, basis, slopes, residual, g, zh, zl, qh, ql, pre, c, m, t, w_m, w_o, feat, x):
    out = lambda s, t: jax.ShapeDtypeStruct(s, t)
    smem = pl.BlockSpec(memory_space=pltpu.SMEM)
    return pl.pallas_call(
        grad_kernel,
        name="weighted",
        grid=(STEPSG,),
        in_specs=[smem, smem, glanes(1), glanes(1), glanes(1), GVEC, glanes(NB), glanes(NB), whole((8, 128))]
        + [whole((8, GHOST))] * 4 + [glanes(H)] * 8
        + [whole((H, H)), whole((1, H)), whole((ATOMS, F)), whole((GHOST, F))] + [whole((GHOST, F))] * 3,
        out_specs=[whole((HALF, 128))] * 2,
        out_shape=[pltpu.VMEM((HALF, 128), f32)] * 2,
        scratch_shapes=[pltpu.VMEM((16, 384), f32), pltpu.VMEM((H, 2 * H), bf16), pltpu.VMEM((H, 128), f32)]
        + [pltpu.VMEM((H, BG), bf16) for _ in range(8)]
        + [pltpu.VMEM((H, H), f32), pltpu.VMEM((416, H), f32), pltpu.VMEM((16, H), f32), pltpu.VMEM((H, 128), f32)],
        compiler_params=params(GRAD),
        cost_estimate=pl.CostEstimate(flops=2 * 10**10, bytes_accessed=26 << 20, transcendentals=0),
    )(live, core, fi, se, sp, vec, basis, slopes, residual, *g, zh, zl, qh, ql, pre, c, m, t, w_m, w_o, feat, *x)


def unpack_kernel(core, mine, other, ga, gb, gr, gs, gm, go):
    def write(ref, half):
        for b in range(2):
            lo = (2 * half + b) * 128
            for at, n, o in ((0, 128, ga), (128, 128, gb), (256, 8, gr), (264, 16, gs), (280, 512, gm), (792, 1, go)):
                o[:, lo:lo + 128] = ref[SEG * b + at:SEG * b + at + n, :]

    @pl.when(core[0] == 0)
    def _():
        write(mine, 0)
        write(other, 1)

    @pl.when(core[0] != 0)
    def _():
        write(mine, 1)
        write(other, 0)


def unpack(core, mine, other):
    out = lambda r: jax.ShapeDtypeStruct((r, H), f32)
    return pl.pallas_call(
        unpack_kernel,
        name="unpack",
        in_specs=[pl.BlockSpec(memory_space=pltpu.SMEM), whole((HALF, 128)), whole((HALF, 128))],
        out_shape=[out(128), out(128), out(8), out(16), out(512), out(1)],
        compiler_params=params(8 << 20),
    )(core, mine, other)


def moved(block, delta):
    nx, ny = (math.prod(lax.axis_size(a) for a in axes) for axes in (BX, BY))
    route = [(a * ny + b, (a + delta[0]) % nx * ny + (b + delta[1]) % ny) for a in range(nx) for b in range(ny)]
    return lax.ppermute(block, AXES, route)


DIRS = ((1, 0), (0, 1), (1, 1), (1, -1))


def exchange(blocks, step):
    return [moved(block, (step * dx, step * dy)) for block, (dx, dy) in zip(blocks, DIRS)]


def sum_over_slice(mine, theirs):
    swap = [(0, 1), (1, 0)]
    plane = ("zl", "xh", "xl", "y")
    n = math.prod(lax.axis_size(a) for a in plane)
    depth = lax.axis_size("zh")
    part = (mine + lax.ppermute(theirs, "c", swap)).reshape(n, HALF // n, 128)
    part = jnp.sum(lax.all_to_all(part, plane, 0, 0, tiled=True), axis=0)
    part = jnp.broadcast_to(part[None], (depth,) + part.shape)
    part = jnp.sum(lax.all_to_all(part, "zh", 0, 0, tiled=True), axis=0)
    part = jnp.broadcast_to(part[None], (n,) + part.shape)
    full = lax.all_to_all(part, plane, 0, 0, tiled=True).reshape(HALF, 128)
    return full, lax.ppermute(full, "c", swap)


def local(features, send_list, pair_first, pair_second, pair_species, pair_vector, live_pairs, force_target,
          w_a, w_b, w_radial, species_table, w_mid, w_out):
    feat = features[0, 0]
    sends = send_list.reshape(4, 1, GHOST)
    fi = pair_first[0]
    se = pair_second[0]
    sp = pair_species[0]
    vec = pair_vector.reshape(3, 1, PAIRS)
    live = live_pairs.reshape(1)
    core = lax.axis_index("c").reshape(1)
    weights = (w_a, w_b, w_radial, species_table, w_mid, w_out[None])
    near = lambda xs: [pltpu.with_memory_space_constraint(x, pltpu.VMEM) for x in xs]
    ghosts = exchange(lend(feat, sends), -1)
    zh, zl, qh, ql, pre, c, m, t, basis, slopes, eloc, *parts = forward(
        live, fi, se, sp, vec, feat, near(ghosts), weights)
    forces, residual, *lent = force_step(eloc, exchange(parts, 1), sends, force_target.reshape(3, 1, ATOMS))
    ghost_res = exchange(lent, -1)
    mine, theirs = weighted(live, core, fi, se, sp, vec, basis, slopes, residual, near(ghost_res),
                            zh, zl, qh, ql, pre, c, m, t, w_mid, weights[5], feat, ghosts)
    mine, other = sum_over_slice(mine, theirs)
    ga, gb, gr, gs, gm, go = unpack(core, mine, other)
    return (forces.reshape(1, 1, 3, ATOMS), ga, gb, gr, gs, gm, go[0])


def solution(mesh):
    inner = Mesh(mesh.devices.reshape(4, 2, 2, 2, 4, 2), AXES)
    four = P(BX, BY, None, None)
    three = P(BX, BY, None)
    return jax.shard_map(
        local,
        mesh=inner,
        in_specs=(four, four, three, three, three, four, P(BX, BY), four, P(), P(), P(), P(), P(), P()),
        out_specs=(four, P(), P(), P(), P(), P(), P()),
        check_vma=False,
    )
```

```python
import functools
import math

import jax
import jax.numpy as jnp
from jax import lax
from jax.experimental import pallas as pl
from jax.experimental.pallas import tpu as pltpu
from jax.sharding import Mesh
from jax.sharding import PartitionSpec as P

RCUT = 5.0
AXES = ("zh", "zl", "xh", "xl", "y", "c")
BX = ("zh", "zl", "xh")
BY = ("xl", "y", "c")
ATOMS = 128
GHOST = 32
PAIRS = 2048
H = 512
F = 128
NB = 8
NS = 16
B = 512
W = 256
BG = 512
WG = 256
SEG = 800
HALF = 1792
STEPS = PAIRS // B
STEPSG = PAIRS // BG
f32 = jnp.float32
bf16 = jnp.bfloat16
HI = lax.Precision.HIGHEST
VMEM = 64_000_000
FWD = 56 << 20
GRAD = 56 << 20
NT = (((1,), (1,)), ((), ()))
NN = (((1,), (0,)), ((), ()))


def split(x):
    h = x.astype(bf16)
    return h, (x - h.astype(f32)).astype(bf16)


def dot(a, b, dims=NN, precision=None):
    return lax.dot_general(a, b, dims, precision=precision, preferred_element_type=f32)


def sigmoid(x):
    return 0.5 * jnp.tanh(0.5 * x) + 0.5


def whole(shape):
    return pl.BlockSpec(shape, lambda *_: (0,) * len(shape))


def lanes(rows):
    return pl.BlockSpec((rows, B), lambda i: (0, i))


def glanes(rows):
    return pl.BlockSpec((rows, BG), lambda i: (0, i))


def params(limit=VMEM):
    return pltpu.CompilerParams(vmem_limit_bytes=limit)


def send_row(sends, row):
    for d in range(4):
        row[:, GHOST * d:GHOST * (d + 1)] = sends[d]
    return jnp.where(lax.broadcasted_iota(jnp.int32, (ATOMS, 128), 0) == row[...], 1.0, 0.0)


def lend_kernel(feat, sends, l0, l1, l2, l3, row):
    rows = dot(send_row(sends, row).T, feat[...], NN, HI)
    rows = [rows[GHOST * d:GHOST * (d + 1), :] for d in range(4)]
    for d, l in enumerate((l0, l1, l2, l3)):
        l[...] = rows[d]


def lend(feat, sends):
    return pl.pallas_call(
        lend_kernel,
        name="lend",
        out_shape=[pltpu.VMEM((GHOST, F), f32)] * 4,
        scratch_shapes=[pltpu.VMEM((1, 128), jnp.int32)],
        compiler_params=params(56 << 20),
    )(feat, sends)


def onehots(fi, se):
    n = fi.shape[1]
    a = jnp.where(lax.broadcasted_iota(jnp.int32, (128, n), 0) == fi, 1.0, 0.0).astype(bf16)
    b = jnp.where(lax.broadcasted_iota(jnp.int32, (256, n), 0) == se, 1.0, 0.0).astype(bf16)
    return jnp.concatenate([a, b], 0)


def species_hot(sp):
    return jnp.where(lax.broadcasted_iota(jnp.int32, (NS, sp.shape[1]), 0) == sp, 1.0, 0.0)


def parts_of(x):
    h = x.astype(bf16).astype(f32)
    return h, x - h


def tile(x, n):
    return jnp.concatenate([x] * (n // 128), 1)


def forward_kernel(live, fi, se, sp, vec, feat, gx, g1, g2, g3, w_a, w_b, w_r, w_s, w_m, w_o,
                   zh, zl, qh, ql, pre_out, c_out, m_out, t_out, basis, slopes, eloc, p0, p1, p2, p3,
                   tab, wt, wr3, wob, acc):
    i = pl.program_id(0)

    @pl.when(i == 0)
    def _():
        wt[:, 0:H], wt[:, H:2 * H] = split(w_m[...].T)
        table = jnp.concatenate([feat[...], gx[...], g1[...], g2[...], g3[...]], 0)
        tab[:, 0:128], tab[:, 384:512] = split(dot(w_a[...].T, feat[...], NT, HI))
        tab[:, 128:384], tab[:, 512:768] = split(dot(w_b[...].T, table, NT, HI))
        ws, wr = w_s[...], w_r[...]
        wide = jnp.concatenate([ws, wr, wr, ws, wr, jnp.zeros((72, H), f32)], 0).T
        h, l = parts_of(wide)
        col = lax.broadcasted_iota(jnp.int32, (H, 128), 1)
        tab[:, 768:896] = jnp.where(col < 32, h, l).astype(bf16)
        h, l = parts_of(jnp.concatenate([wr, wr, wr, jnp.zeros((104, H), f32)], 0).T)
        wr3[...] = jnp.where(col < 16, h, l).astype(bf16)
        wob[...] = jnp.broadcast_to(w_o[...], (128, H)).T
        acc[...] = jnp.zeros_like(acc)

    v = jnp.concatenate([vec[0], vec[1], vec[2]], 0)
    square = jnp.sum(v * v, axis=0, keepdims=True) + 1.0
    radius = jnp.sqrt(square)
    order = (lax.broadcasted_iota(jnp.int32, (NB, 1), 0) + 1).astype(f32) * (math.pi / RCUT)
    phase = order * radius
    sn = jnp.sin(phase)
    cs = jnp.cos(phase)
    base = sn / radius
    rate = (order * cs / radius - sn / square) / radius
    basis[...] = base
    slopes[...] = rate
    kinds = species_hot(sp[...])
    bh, bl = parts_of(base)
    ones = jnp.concatenate([kinds, bh, bl, kinds, bh, jnp.zeros((72, B), f32)], 0).astype(bf16)
    sh, sl = parts_of(rate)
    bsr = jnp.concatenate([sh, sl, sh, jnp.zeros((104, B), f32)], 0).astype(bf16)
    v8 = jnp.concatenate([v, jnp.zeros((5, B), f32)], 0)
    oh = onehots(fi[...], se[...])
    w3 = jnp.concatenate([wt[...], wt[:, 0:H]], 1)
    spans = [slice(lo, lo + W) for lo in range(0, B, W)]

    def enter(k):
        pre = dot(tab[...], jnp.concatenate([oh[:, k], oh[:, k], ones[:, k]], 0))
        return pre, dot(wr3[...], bsr[:, k])

    def first(k, pre, c):
        for r in range(0, H, 16):
            x = pre[r:r + 16]
            cc = c[r:r + 16]
            s = sigmoid(x)
            z = x * s
            pre_out[r:r + 16, k] = x
            c_out[r:r + 16, k] = cc
            zh[r:r + 16, k], zl[r:r + 16, k] = split(z)
            qh[r:r + 16, k], ql[r:r + 16, k] = split((s + z * (1.0 - s)) * cc)

    def middle(k):
        m = dot(w3, jnp.concatenate([zh[:, k], zh[:, k], zl[:, k]], 0))
        return m, dot(w3, jnp.concatenate([qh[:, k], qh[:, k], ql[:, k]], 0))

    def last(k, m, t):
        total = jnp.zeros((16, W), f32)
        for r in range(0, H, 16):
            x = m[r:r + 16]
            tt = t[r:r + 16]
            s = sigmoid(x)
            z = x * s
            m_out[r:r + 16, k] = x
            t_out[r:r + 16, k] = tt
            total = total + tile(wob[r:r + 16, :], W) * ((s + z * (1.0 - s)) * tt)
        return jnp.sum(total, axis=0, keepdims=True)

    pres = [enter(k) for k in spans]
    mids = []
    for k, (pre, c) in zip(spans, pres):
        first(k, pre, c)
        mids.append(middle(k))
    slope = jnp.concatenate([last(k, m, t) for k, (m, t) in zip(spans, mids)], 1)
    slot = lax.broadcasted_iota(jnp.int32, (1, B), 1) + i * B
    coupling = jnp.where(slot < live[0], slope, 0.0)
    lhs = jnp.concatenate(parts_of(coupling * v8), 0).astype(bf16)
    acc[...] += dot(lhs, oh, NT)

    @pl.when(i == STEPS - 1)
    def _():
        e = acc[0:8, :] + acc[8:16, :]
        eloc[...] = e[:, 0:128] - e[:, 128:256]
        parts = [-e[:, 256 + 32 * d:288 + 32 * d] for d in range(4)]
        for d, p in enumerate((p0, p1, p2, p3)):
            p[...] = parts[d]


VEC = pl.BlockSpec((3, 1, B), lambda i: (0, 0, i))
GVEC = pl.BlockSpec((3, 1, BG), lambda i: (0, 0, i))
WEIGHTS = [whole((F, H)), whole((F, H)), whole((NB, H)), whole((NS, H)), whole((H, H)), whole((1, H))]


def forward(live, fi, se, sp, vec, feat, ghosts, weights):
    out = lambda s, t: jax.ShapeDtypeStruct(s, t)
    big = (H, PAIRS)
    return pl.pallas_call(
        forward_kernel,
        name="forward",
        grid=(STEPS,),
        in_specs=[pl.BlockSpec(memory_space=pltpu.SMEM), lanes(1), lanes(1), lanes(1), VEC, whole((ATOMS, F))]
        + [whole((GHOST, F))] * 4 + WEIGHTS,
        out_specs=[lanes(H)] * 8 + [lanes(NB)] * 2 + [whole((8, 128))] + [whole((8, GHOST))] * 4,
        out_shape=[out(big, bf16)] * 4 + [out(big, f32)] * 4 + [out((NB, PAIRS), f32)] * 2
        + [pltpu.VMEM((8, 128), f32)] + [pltpu.VMEM((8, GHOST), f32)] * 4,
        scratch_shapes=[pltpu.VMEM((H, 896), bf16), pltpu.VMEM((H, 2 * H), bf16), pltpu.VMEM((H, 128), bf16),
                        pltpu.VMEM((H, 128), f32), pltpu.VMEM((16, 384), f32)],
        compiler_params=params(FWD),
        cost_estimate=pl.CostEstimate(flops=10**10, bytes_accessed=36 << 20, transcendentals=2 * H * PAIRS),
    )(live, fi, se, sp, vec, feat, *ghosts, *weights)


def force_kernel(eloc, rx, r1, r2, r3, sends, target, forces, residual, l0, l1, l2, l3, got, row):
    for d, r in enumerate((rx[...], r1[...], r2[...], r3[...])):
        got[:, GHOST * d:GHOST * (d + 1)] = r
    lent = send_row(sends, row)
    total = eloc[...] + dot(got[...], lent, NT, HI)
    goal = jnp.concatenate([target[0], target[1], target[2]], 0)
    for k in range(3):
        forces[k] = total[k:k + 1, :]
    res = (total[0:3, :] - goal) / ATOMS
    res = jnp.concatenate([res, jnp.zeros((5, ATOMS), f32)], 0)
    residual[...] = res
    picked = dot(res, lent, NN, HI)
    picked = [picked[:, GHOST * d:GHOST * (d + 1)] for d in range(4)]
    for d, l in enumerate((l0, l1, l2, l3)):
        l[...] = picked[d]


def force_step(eloc, returned, sends, target):
    out = lambda s: jax.ShapeDtypeStruct(s, f32)
    return pl.pallas_call(
        force_kernel,
        name="forces",
        out_shape=[out((3, 1, 128)), pltpu.HBM((8, 128), f32)] + [out((8, GHOST))] * 4,
        scratch_shapes=[pltpu.VMEM((8, 128), f32), pltpu.VMEM((1, 128), jnp.int32)],
        compiler_params=params(4 << 20),
    )(eloc, *returned, sends, target)


def grad_kernel(live, core, fi, se, sp, vec, basis, slopes, residual, gx, g1, g2, g3,
                zh, zl, qh, ql, pre, c, m_in, t_in, w_m, w_o, feat, xx, x1, x2, x3,
                mine, theirs,
                table, ww, wob, ah, al, bh, bl, ph, plo, ch, cl, wacc, gacc, racc, oacc):
    i = pl.program_id(0)

    @pl.when(i == 0)
    def _():
        def put(lo, x):
            h, l = parts_of(x)
            table[0:8, lo:lo + x.shape[1]] = h
            table[8:16, lo:lo + x.shape[1]] = l
        put(0, residual[...])
        put(128, -residual[...])
        for d, g in enumerate((gx[...], g1[...], g2[...], g3[...])):
            put(256 + GHOST * d, -g)
        ww[:, 0:H], ww[:, H:2 * H] = split(w_m[...])
        wob[...] = jnp.broadcast_to(w_o[...], (128, H)).T
        wacc[...] = jnp.zeros_like(wacc)
        gacc[...] = jnp.zeros_like(gacc)
        racc[...] = jnp.zeros_like(racc)
        oacc[...] = jnp.zeros_like(oacc)

    oh = onehots(fi[...], se[...])
    gap = dot(table[...].astype(bf16), oh)
    gap = gap[0:8] + gap[8:16]
    weight = gap[0:1] * vec[0] + gap[1:2] * vec[1] + gap[2:3] * vec[2]
    slot = lax.broadcasted_iota(jnp.int32, (1, BG), 1) + i * BG
    weight = jnp.broadcast_to(jnp.where(slot < live[0], weight, 0.0), (16, BG))
    w3 = jnp.concatenate([ww[...], ww[:, 0:H]], 1)
    rows = jnp.concatenate(
        [oh, jnp.concatenate([species_hot(sp[...]), *parts_of(basis[...])], 0).astype(bf16)], 0)
    rates = jnp.concatenate(parts_of(slopes[...]), 0).astype(bf16)

    def enter(k):
        wk = weight[:, k]
        for r in range(0, H, 16):
            x = m_in[r:r + 16, k]
            tt = t_in[r:r + 16, k]
            w = tile(wob[r:r + 16, :], WG)
            s = sigmoid(x)
            n = 1.0 - s
            d1 = (s + x * s * n) * wk
            d2 = s * n * (2.0 + x * (n - s)) * tt
            ah[r:r + 16, k], al[r:r + 16, k] = split(w * (d2 * wk))
            bh[r:r + 16, k], bl[r:r + 16, k] = split(w * d1)
            y = d1 * tt
            oacc[r:r + 16, :] += sum(y[:, j:j + 128] for j in range(0, WG, 128))

    def back(k):
        return (dot(w3, jnp.concatenate([ah[:, k], ah[:, k], al[:, k]], 0)),
                dot(w3, jnp.concatenate([bh[:, k], bh[:, k], bl[:, k]], 0)))

    def outer(k):
        wacc[...] += dot(
            jnp.concatenate([zh[:, k], zh[:, k], zl[:, k], qh[:, k], qh[:, k], ql[:, k]], 1),
            jnp.concatenate([ah[:, k], al[:, k], ah[:, k], bh[:, k], bl[:, k], bh[:, k]], 1), NT)

    def leave(k, zb, qb):
        for r in range(0, H, 16):
            x = pre[r:r + 16, k]
            s = sigmoid(x)
            n = 1.0 - s
            d1 = s + x * s * n
            d2 = s * n * (2.0 + x * (n - s))
            q = qb[r:r + 16]
            ph[r:r + 16, k], plo[r:r + 16, k] = split(zb[r:r + 16] * d1 + q * (c[r:r + 16, k] * d2))
            ch[r:r + 16, k], cl[r:r + 16, k] = split(q * d1)

    def sums(k):
        gacc[...] += dot(jnp.concatenate([rows[:, k], rows[:, k]], 1),
                         jnp.concatenate([ph[:, k], plo[:, k]], 1), NT)
        racc[...] += dot(jnp.concatenate([rates[:, k], rates[:, k]], 1),
                         jnp.concatenate([ch[:, k], cl[:, k]], 1), NT)

    spans = [slice(lo, lo + WG) for lo in range(0, BG, WG)]
    enter(spans[0])
    for n, k in enumerate(spans):
        got = back(k)
        if n + 1 < len(spans):
            enter(spans[n + 1])
        if n:
            sums(spans[n - 1])
        outer(k)
        leave(k, *got)
    sums(spans[-1])

    @pl.when(i == STEPSG - 1)
    def _():
        ga = dot(feat[...].T, gacc[0:128, :], NN, HI)
        rest = jnp.concatenate([feat[...], xx[...], x1[...], x2[...], x3[...]], 0)
        gb = dot(rest.T, gacc[128:384, :], NN, HI)
        gr = gacc[400:408, :] + gacc[408:416, :] + racc[0:8, :] + racc[8:16, :]
        go = dot(jnp.ones((8, 128), f32), oacc[...], NT, HI)
        pieces = ((0, ga), (128, gb), (256, gr), (264, gacc[384:400, :]), (280, wacc[...]), (792, go))

        def write(ref, half):
            for b in range(2):
                at0 = (2 * half + b) * 128
                for at, piece in pieces:
                    ref[SEG * b + at:SEG * b + at + piece.shape[0], :] = piece[:, at0:at0 + 128]
            ref[2 * SEG:HALF, :] = jnp.zeros((HALF - 2 * SEG, 128), f32)

        @pl.when(core[0] == 0)
        def _():
            write(mine, 0)
            write(theirs, 1)

        @pl.when(core[0] != 0)
        def _():
            write(mine, 1)
            write(theirs, 0)


def weighted(live, core, fi, se, sp, vec, basis, slopes, residual, g, zh, zl, qh, ql, pre, c, m, t, w_m, w_o, feat, x):
    out = lambda s, t: jax.ShapeDtypeStruct(s, t)
    smem = pl.BlockSpec(memory_space=pltpu.SMEM)
    return pl.pallas_call(
        grad_kernel,
        name="weighted",
        grid=(STEPSG,),
        in_specs=[smem, smem, glanes(1), glanes(1), glanes(1), GVEC, glanes(NB), glanes(NB), whole((8, 128))]
        + [whole((8, GHOST))] * 4 + [glanes(H)] * 8
        + [whole((H, H)), whole((1, H)), whole((ATOMS, F)), whole((GHOST, F))] + [whole((GHOST, F))] * 3,
        out_specs=[whole((HALF, 128))] * 2,
        out_shape=[pltpu.VMEM((HALF, 128), f32)] * 2,
        scratch_shapes=[pltpu.VMEM((16, 384), f32), pltpu.VMEM((H, 2 * H), bf16), pltpu.VMEM((H, 128), f32)]
        + [pltpu.VMEM((H, BG), bf16) for _ in range(8)]
        + [pltpu.VMEM((H, H), f32), pltpu.VMEM((416, H), f32), pltpu.VMEM((16, H), f32), pltpu.VMEM((H, 128), f32)],
        compiler_params=params(GRAD),
        cost_estimate=pl.CostEstimate(flops=2 * 10**10, bytes_accessed=26 << 20, transcendentals=0),
    )(live, core, fi, se, sp, vec, basis, slopes, residual, *g, zh, zl, qh, ql, pre, c, m, t, w_m, w_o, feat, *x)


def unpack_kernel(core, mine, other, ga, gb, gr, gs, gm, go):
    def write(ref, half):
        for b in range(2):
            lo = (2 * half + b) * 128
            for at, n, o in ((0, 128, ga), (128, 128, gb), (256, 8, gr), (264, 16, gs), (280, 512, gm), (792, 1, go)):
                o[:, lo:lo + 128] = ref[SEG * b + at:SEG * b + at + n, :]

    @pl.when(core[0] == 0)
    def _():
        write(mine, 0)
        write(other, 1)

    @pl.when(core[0] != 0)
    def _():
        write(mine, 1)
        write(other, 0)


def unpack(core, mine, other):
    out = lambda r: jax.ShapeDtypeStruct((r, H), f32)
    return pl.pallas_call(
        unpack_kernel,
        name="unpack",
        in_specs=[pl.BlockSpec(memory_space=pltpu.SMEM), whole((HALF, 128)), whole((HALF, 128))],
        out_shape=[out(128), out(128), out(8), out(16), out(512), out(1)],
        compiler_params=params(8 << 20),
    )(core, mine, other)


def moved(block, delta):
    nx, ny = (math.prod(lax.axis_size(a) for a in axes) for axes in (BX, BY))
    route = [(a * ny + b, (a + delta[0]) % nx * ny + (b + delta[1]) % ny) for a in range(nx) for b in range(ny)]
    return lax.ppermute(block, AXES, route)


DIRS = ((1, 0), (0, 1), (1, 1), (1, -1))


def exchange(blocks, step):
    return [moved(block, (step * dx, step * dy)) for block, (dx, dy) in zip(blocks, DIRS)]


def sum_over_slice(mine, theirs):
    swap = [(0, 1), (1, 0)]
    plane = ("zl", "xh", "xl", "y")
    n = math.prod(lax.axis_size(a) for a in plane)
    depth = lax.axis_size("zh")
    part = (mine + lax.ppermute(theirs, "c", swap)).reshape(n, HALF // n, 128)
    part = jnp.sum(lax.all_to_all(part, plane, 0, 0, tiled=True), axis=0)
    part = jnp.broadcast_to(part[None], (depth,) + part.shape)
    part = jnp.sum(lax.all_to_all(part, "zh", 0, 0, tiled=True), axis=0)
    part = jnp.broadcast_to(part[None], (n,) + part.shape)
    full = lax.all_to_all(part, plane, 0, 0, tiled=True).reshape(HALF, 128)
    return full, lax.ppermute(full, "c", swap)


def local(features, send_list, pair_first, pair_second, pair_species, pair_vector, live_pairs, force_target,
          w_a, w_b, w_radial, species_table, w_mid, w_out):
    feat = features[0, 0]
    sends = send_list.reshape(4, 1, GHOST)
    fi = pair_first[0]
    se = pair_second[0]
    sp = pair_species[0]
    vec = pair_vector.reshape(3, 1, PAIRS)
    live = live_pairs.reshape(1)
    core = lax.axis_index("c").reshape(1)
    weights = (w_a, w_b, w_radial, species_table, w_mid, w_out[None])
    near = lambda xs: [pltpu.with_memory_space_constraint(x, pltpu.VMEM) for x in xs]
    ghosts = exchange(lend(feat, sends), -1)
    zh, zl, qh, ql, pre, c, m, t, basis, slopes, eloc, *parts = forward(
        live, fi, se, sp, vec, feat, near(ghosts), weights)
    forces, residual, *lent = force_step(eloc, exchange(parts, 1), sends, force_target.reshape(3, 1, ATOMS))
    ghost_res = exchange(lent, -1)
    mine, theirs = weighted(live, core, fi, se, sp, vec, basis, slopes, residual, near(ghost_res),
                            zh, zl, qh, ql, pre, c, m, t, w_mid, weights[5], feat, ghosts)
    mine, other = sum_over_slice(mine, theirs)
    ga, gb, gr, gs, gm, go = unpack(core, mine, other)
    return (forces.reshape(1, 1, 3, ATOMS), ga, gb, gr, gs, gm, go[0])


def solution(mesh):
    inner = Mesh(mesh.devices.reshape(4, 2, 2, 2, 4, 2), AXES)
    four = P(BX, BY, None, None)
    three = P(BX, BY, None)
    return jax.shard_map(
        local,
        mesh=inner,
        in_specs=(four, four, three, three, three, four, P(BX, BY), four, P(), P(), P(), P(), P(), P()),
        out_specs=(four, P(), P(), P(), P(), P(), P()),
        check_vma=False,
    )
```
